256 devices in a mesh: space: 32 (over y, x, core), chan: 8 (over z).
Axes of the slice: x: 4, y: 4, z: 8, core: 2. Of those that a mesh axis runs over, the one named last changes fastest.
Arguments:
- positions: float32 [3, 16384], P(None, 'space'), may hold values from -6 to 6
- features: float32 [512, 16384], P('chan', 'space'), may hold values from -6 to 6
- block_counts: int32 [128], P('space'), may hold values from 64 to 128
- pair_table: int32 [3, 2048], P(None, 'space'), may hold values from 0 to 127, as said below
- in_weight: float32 [2, 512, 512], P(None, 'chan'), may hold values from -0.25 to 0.25
- filter_weight: float32 [2, 8, 512], P(None, None, 'chan'), may hold values from -0.125 to 0.125
- mix_weight: float32 [2, 512, 512], P(None, None, 'chan'), may hold values from -0.25 to 0.25
Outputs:
- updated: float32 [512, 16384], P('chan', 'space')
The draws below stay inside these ranges and needn't reach their ends.
Inputs may be any that keep to these rules, and one draw needn't show every extreme that they name: `pair_table`: blocks n * 4 to (n + 1) * 4 - 1 lie on device n along space. In slot p of device d's pair slots the first block is one of device d's blocks and the second a block of device (d + o) mod the number of devices along space, with o from 0 to 8; the third row is 0 or 1. On every device the first 9 slots are live and slot o (o = 0 .. 8) names a second block on device d + o; any live slots follow them, empty slots come last.
All inputs are finite; a program needn't handle non-finite values.
Results may differ from the reference program's by a relative error of at most 0.0003.
Values sent between devices are 32-bit elements; how exact they have to be, the bound alone decides.
No kernel may reach another device: no remote copies, remote signals or barrier semaphores. Data moves between devices by JAX's collectives and lax.ppermute only.
A program may use at most 64 MiB of HBM per device.

```python
import jax
import jax.numpy as jnp
from jax import lax

F = 512
K = 8
BLK = 128
LAYERS = 2
PPB = 16
B_DEV = 4
PAIR_DEV = 64
NBLK = 128
ATOMS = 16384
NPAIRS = 2048


def draw_pair_table(key, part):
    spatial = NPAIRS // PAIR_DEV
    reach_dev = spatial // 4
    key_shift, key_first, key_second, key_alive = jax.random.split(jax.random.fold_in(key, 17), 4)
    position_id = jnp.arange(NPAIRS, dtype=jnp.int32)
    device = position_id // PAIR_DEV
    slot_at = position_id % PAIR_DEV
    shifts = jax.random.randint(key_shift, (NPAIRS,), 0, reach_dev + 1)
    shifts = jnp.where(slot_at <= reach_dev, slot_at, shifts)
    first_block = device * B_DEV + jax.random.randint(key_first, (NPAIRS,), 0, B_DEV)
    second_block = (device + shifts) % spatial * B_DEV + jax.random.randint(key_second, (NPAIRS,), 0, B_DEV)
    live_count = jax.random.randint(key_alive, (spatial,), PAIR_DEV // 3, PAIR_DEV + 1)
    live_count = jnp.maximum(live_count, reach_dev + 1)
    alive_flag = (slot_at < live_count[device]).astype(jnp.int32)
    return jnp.stack([first_block, second_block, alive_flag]).astype(jnp.int32)


def with_ends(values, key, least, high):
    shape = values.shape
    index_at = [jax.random.randint(jax.random.fold_in(key, axis), (), 0, shape[axis]) for axis in range(len(shape))]
    values = values.at[tuple(index_at)].set(least)
    longest = shape.index(max(shape))
    index_at[longest] = (index_at[longest] + 1) % shape[longest]
    return values.at[tuple(index_at)].set(high)


def block_levels(own_key, shape, cuts, low, top_value):
    gain, own = 1.0, jax.random.fold_in(own_key, 6)
    for axis_at, parts in cuts:
        draws = jnp.exp(jax.random.uniform(jax.random.fold_in(own, axis_at), (parts,), jnp.float32, low / len(cuts), top_value / len(cuts)))
        gain = gain * jnp.repeat(draws, shape[axis_at] // parts).reshape([-1 if axis == axis_at else 1 for axis in range(len(shape))])
    return gain


def gaussian(rng, shape, scale, reach, cuts=(), held_as=jnp.bfloat16):
    drawn = jax.random.normal(rng, shape, jnp.float32) * scale
    if len(cuts) > 0:
        drawn = block_levels(rng, shape, cuts, -0.22, 0.18) * drawn
    return jnp.clip(drawn, min=-reach, max=reach).astype(held_as)


def setup_inputs(seed: int = 0) -> dict:
    keys = jax.random.split(jax.random.key(seed), 8)
    positions = gaussian(keys[0], (3, ATOMS), 1.5, 6.0, ((1, 32),), jnp.float32)
    features = gaussian(keys[1], (F, ATOMS), 1.0, 6.0, ((0, 8), (1, 32)), jnp.float32)
    block_counts = with_ends(jax.random.randint(keys[2], (NBLK,), BLK // 2, BLK + 1), jax.random.fold_in(keys[2], 1), BLK // 2, BLK).astype(jnp.int32)
    pair_table = draw_pair_table(jax.random.fold_in(keys[7], 71), 0)
    in_weight = gaussian(keys[4], (LAYERS, F, F), F ** -0.5, 0.25, ((1, 8),), jnp.float32)
    filter_weight = gaussian(keys[5], (LAYERS, K, F), (PPB * BLK) ** -0.5, 0.125, ((2, 8),), jnp.float32)
    mix_weight = gaussian(keys[6], (LAYERS, F, F), F ** -0.5, 0.25, ((2, 8),), jnp.float32)
    return {"positions": positions, "features": features, "block_counts": block_counts, "pair_table": pair_table, "in_weight": in_weight, "filter_weight": filter_weight, "mix_weight": mix_weight}


cutoff_radius = 6.0
gamma_width = 1.5

def radial_basis(first_geo, second_geo, keep_pair, same_block):
    offsets = first_geo[..., :3, :, None] - second_geo[..., :3, None, :]
    squared = lax.optimization_barrier(jnp.sum(offsets * offsets, axis=-3))
    distance = jnp.sqrt(squared)
    envelope = jnp.where(distance < cutoff_radius, 0.5 * (jnp.cos(jnp.pi * distance / cutoff_radius) + 1.0), 0.0)
    extent = distance.shape[-1]
    diagonal = (lax.broadcasted_iota(jnp.int32, (extent, extent), 0) == lax.broadcasted_iota(jnp.int32, (extent, extent), 1)).astype(jnp.float32)
    allowed = first_geo[..., 3, :, None] * second_geo[..., 3, None, :] * keep_pair[..., None, None] * (1.0 - same_block[..., None, None] * diagonal)
    centers = jnp.arange(K, dtype=jnp.float32) * (cutoff_radius / (K - 1))
    spread = distance[..., None, :, :] - centers[:, None, None]
    return jnp.exp(-gamma_width * spread * spread) * (envelope * allowed)[..., None, :, :]

def reference(positions, features, block_counts, pair_table, in_weight, filter_weight, mix_weight):
    valid = (jnp.arange(BLK, dtype=jnp.int32)[None, :] < block_counts[:, None]).astype(jnp.float32).reshape(1, -1)
    geometry = jnp.concatenate([positions, valid], axis=0)
    state = features
    for layer in range(LAYERS):
        mapped = jnp.dot(in_weight[layer], state, precision=lax.Precision.HIGHEST, preferred_element_type=jnp.float32)
        weights_f = filter_weight[layer]

        def pair_step(collected, column, mapped=mapped, weights_f=weights_f):
            first_start = (column[0] * BLK).astype(jnp.int32)
            second_start = (column[1] * BLK).astype(jnp.int32)
            keep_now = column[2].astype(jnp.float32)
            same_now = (column[0] == column[1]).astype(jnp.float32)
            first_geo = lax.dynamic_slice_in_dim(geometry, first_start, BLK, 1)
            second_geo = lax.dynamic_slice_in_dim(geometry, second_start, BLK, 1)
            basis = radial_basis(first_geo, second_geo, keep_now, same_now)
            first_feat = weights_f[:, :, None] * lax.dynamic_slice_in_dim(mapped, first_start, BLK, 1)[None]
            second_feat = weights_f[:, :, None] * lax.dynamic_slice_in_dim(mapped, second_start, BLK, 1)[None]
            to_first = jnp.einsum('kcj,kij->ci', second_feat, basis, precision=lax.Precision.HIGHEST)
            to_second = jnp.einsum('kci,kij->cj', first_feat, basis, precision=lax.Precision.HIGHEST) * (1.0 - same_now)
            before = lax.dynamic_slice_in_dim(collected, first_start, BLK, 1)
            collected = lax.dynamic_update_slice_in_dim(collected, before + to_first, first_start, 1)
            before = lax.dynamic_slice_in_dim(collected, second_start, BLK, 1)
            collected = lax.dynamic_update_slice_in_dim(collected, before + to_second, second_start, 1)
            return (collected, None)
        messages, unused = lax.scan(pair_step, jnp.zeros(mapped.shape, jnp.float32), pair_table.T)
        mixed = jnp.dot(mix_weight[layer], messages, precision=lax.Precision.HIGHEST, preferred_element_type=jnp.float32)
        state = state + jax.nn.silu(mixed)
    return state
```

```python
import functools
import math

import jax
import jax.numpy as jnp
from jax import lax
from jax.experimental import pallas as pl
from jax.experimental.pallas import tpu as pltpu
from jax.sharding import PartitionSpec as P

K = 8
LAYERS = 2
BLK = 128
LANES = 128

cutoff_radius = 6.0
gamma_width = 1.5
step_width = cutoff_radius / (K - 1)
MID = 4
FAR = 1000.0

ENVELOPE = (
    0.02777777772845049,
    -0.00018032445737786967,
    4.2799604015759175e-07,
    -5.319790167613903e-10,
    3.90316047548473e-13,
)

VMEM = pltpu.MemorySpace.VMEM
SMEM = pltpu.MemorySpace.SMEM


def shifted(block, axis, distance):
    devices = range(lax.axis_size(axis))
    route = [((i - distance) % len(devices), i) for i in devices]
    return lax.ppermute(block, axis, route)


def split(value):
    high = value.astype(jnp.bfloat16)
    low = (value - high.astype(jnp.float32)).astype(jnp.bfloat16)
    return high, low


def basis_kernel(first_ref, second_ref, count_ref, rows_ref, columns_ref, out_ref, wide, buf, sem):
    blocks = columns_ref.shape[0]
    for block in range(blocks):
        for axis in range(3):
            wide[block * 3 + axis] = jnp.broadcast_to(columns_ref[block, :, axis : axis + 1], (BLK, BLK))
    count = count_ref[0]
    chunk = 32

    def one(pair, carry):
        slot = lax.rem(pair, 2)

        @pl.when(pair >= 2)
        def _():
            pltpu.make_async_copy(buf.at[slot], out_ref.at[pair - 2], sem.at[slot]).wait()

        first, second = first_ref[pair], second_ref[pair]
        same = (first == second).astype(jnp.float32)
        for part in range(BLK // chunk):
            rows = slice(part * chunk, (part + 1) * chunk)
            squared = None
            for axis in range(3):
                offset = wide[first * 3 + axis, rows, :] - rows_ref[second, axis : axis + 1, :]
                squared = offset * offset if squared is None else squared + offset * offset
            here = lax.broadcasted_iota(jnp.int32, (chunk, BLK), 0) + part * chunk
            there = lax.broadcasted_iota(jnp.int32, (chunk, BLK), 1)
            squared = squared + jnp.where(here == there, same * FAR, 0.0)
            squared = jnp.minimum(squared, cutoff_radius * cutoff_radius)
            distance = squared * lax.rsqrt(jnp.maximum(squared, 1e-20))
            bell = ENVELOPE[4]
            for power in (3, 2, 1, 0):
                bell = bell * squared + ENVELOPE[power]
            bell = bell * (cutoff_radius * cutoff_radius - squared)
            bell = bell * bell
            away = distance - MID * step_width
            middle = bell * jnp.exp(away * away * -gamma_width)
            up = jnp.exp(away * (2.0 * gamma_width * step_width))
            down = jnp.exp(away * (-2.0 * gamma_width * step_width))

            def keep(k, value):
                high, low = split(value)
                buf[slot, 0, k * BLK + part * chunk : k * BLK + (part + 1) * chunk, :] = high
                buf[slot, 1, k * BLK + part * chunk : k * BLK + (part + 1) * chunk, :] = low

            keep(MID, middle)
            value = middle
            for k in range(MID + 1, K):
                value = value * up
                keep(k, value)
            value = middle
            for k in range(MID - 1, -1, -1):
                value = value * down
                keep(k, value)
        pltpu.make_async_copy(buf.at[slot], out_ref.at[pair], sem.at[slot]).start()
        return carry

    lax.fori_loop(0, count, one, 0)

    @pl.when(count >= 2)
    def _():
        pltpu.make_async_copy(buf.at[lax.rem(count, 2)], out_ref.at[0], sem.at[lax.rem(count, 2)]).wait()

    @pl.when(count >= 1)
    def _():
        pltpu.make_async_copy(buf.at[lax.rem(count + 1, 2)], out_ref.at[0], sem.at[lax.rem(count + 1, 2)]).wait()


def bases(first, second, count, rows, columns):
    pairs = first.shape[0]
    blocks = columns.shape[0]
    return pl.pallas_call(
        basis_kernel,
        out_shape=jax.ShapeDtypeStruct((pairs, 2, K * BLK, BLK), jnp.bfloat16),
        in_specs=[pl.BlockSpec(memory_space=SMEM)] * 3 + [pl.BlockSpec(memory_space=VMEM)] * 2,
        out_specs=pl.BlockSpec(memory_space=pl.ANY),
        scratch_shapes=[
            pltpu.VMEM((blocks * 3, BLK, BLK), jnp.float32),
            pltpu.VMEM((2, 2, K * BLK, BLK), jnp.bfloat16),
            pltpu.SemaphoreType.DMA((2,)),
        ],
        cost_estimate=pl.CostEstimate(flops=pairs * K * BLK * BLK * 10, transcendentals=pairs * BLK * BLK * 4, bytes_accessed=pairs * K * BLK * BLK * 4),
        name="bases",
    )(first, second, count, rows, columns)


def unpack_block(even, odd):
    lane = lax.broadcasted_iota(jnp.int32, even.shape, 1)
    half = LANES // 2
    top = jnp.where(lane < half, even, pltpu.roll(odd, half, 1))
    bottom = jnp.where(lane < half, pltpu.roll(even, half, 1), odd)
    return jnp.concatenate([top, bottom], axis=0)


def pack_block(block):
    channels = block.shape[0]
    top, bottom = block[: channels // 2], block[channels // 2 :]
    lane = lax.broadcasted_iota(jnp.int32, top.shape, 1)
    half = LANES // 2
    even = jnp.where(lane < half, top, pltpu.roll(bottom, half, 1))
    odd = jnp.where(lane < half, pltpu.roll(top, half, 1), bottom)
    return even, odd


def pair_kernel(parts, blocks, *refs):
    first_ref, second_ref, count_ref, weight_ref = refs[:4]
    mapped = refs[4 : 4 + parts]
    basis_ref = refs[4 + parts]
    outs = refs[5 + parts : 5 + 2 * parts]
    scaled, total, buf, sem = refs[5 + 2 * parts :]
    channels = total.shape[1]
    count = count_ref[0]

    def fetch(pair, slot):
        return pltpu.make_async_copy(basis_ref.at[pair], buf.at[slot], sem.at[slot])

    for early in range(2):

        @pl.when(early < count)
        def _():
            fetch(early, early).start()

    for part in range(parts):
        for block in range(blocks):
            feature = unpack_block(mapped[part][2 * block], mapped[part][2 * block + 1])
            for k in range(K):
                high, low = split(feature * jnp.broadcast_to(weight_ref[:, k : k + 1], feature.shape))
                scaled[part * blocks + block, :channels, k * BLK : (k + 1) * BLK] = high
                scaled[part * blocks + block, channels:, k * BLK : (k + 1) * BLK] = low
    total[...] = jnp.zeros_like(total)

    def one(pair, carry):
        slot = lax.rem(pair, 2)
        fetch(pair, slot).wait()
        first, second = first_ref[pair], second_ref[pair]
        differs = (first != second).astype(jnp.float32)
        across = jnp.concatenate([buf[slot, 0], buf[slot, 1]], axis=1)
        to_second = jnp.dot(scaled[first], across, preferred_element_type=jnp.float32)
        down = jnp.concatenate(
            [jnp.concatenate([buf[slot, h, k * BLK : (k + 1) * BLK, :] for k in range(K)], axis=1) for h in range(2)],
            axis=0,
        )
        to_first = lax.dot_general(
            scaled[second], down, (((1,), (1,)), ((), ())), preferred_element_type=jnp.float32
        )

        def fold(whole):
            return (whole[:channels, :BLK] + whole[:channels, BLK:]) + (
                whole[channels:, :BLK] + whole[channels:, BLK:]
            )

        total[first] = total[first] + fold(to_first)
        total[second] = total[second] + fold(to_second) * differs

        @pl.when(pair + 2 < count)
        def _():
            fetch(pair + 2, slot).start()

        return carry

    lax.fori_loop(0, count, one, 0)
    for part in range(parts):
        for block in range(blocks):
            even, odd = pack_block(total[part * blocks + block])
            outs[part][2 * block] = even
            outs[part][2 * block + 1] = odd


def pair_messages(first, second, count, weights, mapped, basis, blocks):
    parts = len(mapped)
    channels = weights.shape[0]
    piece = mapped[0].shape
    return pl.pallas_call(
        functools.partial(pair_kernel, parts, blocks),
        out_shape=[jax.ShapeDtypeStruct(piece, jnp.float32)] * parts,
        in_specs=[pl.BlockSpec(memory_space=SMEM)] * 3
        + [pl.BlockSpec(memory_space=VMEM)] * (1 + parts)
        + [pl.BlockSpec(memory_space=pl.ANY)],
        out_specs=[pl.BlockSpec(memory_space=VMEM)] * parts,
        scratch_shapes=[
            pltpu.VMEM((parts * blocks, 2 * channels, K * BLK), jnp.bfloat16),
            pltpu.VMEM((parts * blocks, channels, BLK), jnp.float32),
            pltpu.VMEM((2, 2, K * BLK, BLK), jnp.bfloat16),
            pltpu.SemaphoreType.DMA((2,)),
        ],
        name="pairs",
    )(first, second, count, weights, *mapped, basis)


def first_map_kernel(weight_ref, state_ref, out_ref):
    product = jnp.dot(
        weight_ref[...], state_ref[...], precision=lax.Precision.HIGHEST, preferred_element_type=jnp.float32
    )
    for block in range(state_ref.shape[1] // BLK):
        even, odd = pack_block(product[:, block * BLK : (block + 1) * BLK])
        out_ref[2 * block] = even
        out_ref[2 * block + 1] = odd


def first_map(weight, state):
    channels = weight.shape[0]
    return pl.pallas_call(
        first_map_kernel,
        out_shape=jax.ShapeDtypeStruct((state.shape[1] // 64, channels // 2, LANES), jnp.float32),
        in_specs=[pl.BlockSpec(memory_space=VMEM)] * 2,
        out_specs=pl.BlockSpec(memory_space=VMEM),
        name="first_map",
    )(weight, state)


def packed_product(weight_ref, value):
    groups = value.shape[0]
    turned = [pltpu.roll(value[g], LANES // 2, 1) for g in range(groups)]
    lower = jnp.concatenate([x for g in range(groups) for x in (value[g], turned[g])], axis=0)
    upper = jnp.concatenate([x for g in range(groups) for x in (turned[g], value[g])], axis=0)
    left = jnp.dot(weight_ref[0], lower, precision=lax.Precision.HIGHEST, preferred_element_type=jnp.float32)
    right = jnp.dot(weight_ref[1], upper, precision=lax.Precision.HIGHEST, preferred_element_type=jnp.float32)
    lane = lax.broadcasted_iota(jnp.int32, left.shape, 1)
    return jnp.where(lane < LANES // 2, left, right).reshape(value.shape)


def update_kernel(last, message_ref, state_ref, mix_ref, *rest):
    mixed = packed_product(mix_ref, message_ref[...])
    state = state_ref[...] + mixed / (1.0 + jnp.exp(-mixed))
    if last:
        rest[0][...] = state
    else:
        map_ref, state_out, mapped_out = rest
        state_out[...] = state
        mapped_out[...] = packed_product(map_ref, state)


def update(message, state, mix, map_next):
    last = map_next is None
    shape = jax.ShapeDtypeStruct(message.shape, jnp.float32)
    operands = (message, state, mix) + (() if last else (map_next,))
    return pl.pallas_call(
        functools.partial(update_kernel, last),
        out_shape=[shape] if last else [shape, shape],
        in_specs=[pl.BlockSpec(memory_space=VMEM)] * len(operands),
        out_specs=[pl.BlockSpec(memory_space=VMEM)] * (1 if last else 2),
        name="update",
    )(*operands)


def unpack_kernel(value_ref, out_ref):
    for block in range(out_ref.shape[1] // BLK):
        out_ref[:, block * BLK : (block + 1) * BLK] = unpack_block(value_ref[2 * block], value_ref[2 * block + 1])


def unpacked(value, shape):
    return pl.pallas_call(
        unpack_kernel,
        out_shape=jax.ShapeDtypeStruct(shape, jnp.float32),
        in_specs=[pl.BlockSpec(memory_space=VMEM)],
        out_specs=pl.BlockSpec(memory_space=VMEM),
        name="unpacked",
    )(value)


def half_rows(weight):
    return weight.reshape(-1, 2, 32, weight.shape[1]).transpose(1, 0, 2, 3).reshape(2, -1, weight.shape[1])


def shards(positions, features, block_counts, pair_table, in_weight, filter_weight, mix_weight):
    spatial = lax.axis_size("space")
    reach_dev = spatial // 4
    own_index = lax.axis_index("space")
    own_chan = lax.axis_index("chan")
    blocks = block_counts.shape[0]
    atoms_dev = positions.shape[1]
    gathered = lax.all_gather(features, "chan", axis=0, tiled=True)

    valid = (lax.broadcasted_iota(jnp.int32, (blocks, BLK), 1) < block_counts[:, None]).reshape(1, atoms_dev)
    geometry = jnp.concatenate([positions, valid.astype(jnp.float32)], axis=0)
    fetched = [geometry]
    for offset in range(1, reach_dev + 1):
        fetched.append(shifted(geometry, "space", -offset))
    everywhere = jnp.stack(fetched)
    there = jnp.concatenate(
        [jnp.where(everywhere[:, 3:4] > 0.5, everywhere[:, :1], -FAR), everywhere[:, 1:]], axis=1
    )
    rows = there.reshape(reach_dev + 1, 4, blocks, BLK).transpose(0, 2, 1, 3).reshape(-1, 4, BLK)
    here = jnp.concatenate([jnp.where(valid, positions[:1], FAR), geometry[1:]], axis=0)
    columns = here.reshape(4, blocks, BLK).transpose(1, 2, 0)

    first = pair_table[0] - own_index * blocks
    second = ((pair_table[1] // blocks - own_index) % spatial) * blocks + pair_table[1] % blocks
    count = jnp.sum(pair_table[2]).reshape(1)
    basis = bases(first, second, count, rows, columns)

    centre = (jnp.arange(K, dtype=jnp.float32) - MID) * step_width
    damp = jnp.exp(-gamma_width * centre * centre)
    weights = filter_weight.transpose(0, 2, 1) * damp

    mapped = first_map(in_weight[0], gathered)
    own_atoms = lax.dynamic_slice_in_dim(gathered, own_chan * 64, 64, 1)
    state = own_atoms.reshape(-1, 2, 32, 64).transpose(0, 2, 1, 3).reshape(-1, 32, LANES)
    mixers = [
        half_rows(lax.all_gather(mix_weight[layer].T, "chan", axis=0, tiled=True).T) for layer in range(LAYERS)
    ]
    mappers = [None] + [
        half_rows(lax.all_gather(in_weight[layer], "chan", axis=0, tiled=True)) for layer in range(1, LAYERS)
    ]
    for layer in range(LAYERS):
        near = [mapped]
        for offset in range(1, reach_dev + 1):
            near.append(shifted(mapped, "space", -offset))
        sent = pair_messages(first, second, count, weights[layer], near, basis, blocks)
        received = sent[0]
        for offset in range(1, reach_dev + 1):
            received = received + shifted(sent[offset], "space", offset)
        message = lax.all_to_all(received, "chan", 0, 0)
        if layer + 1 < LAYERS:
            state, mapped = update(message, state, mixers[layer], mappers[layer + 1])
            mapped = lax.all_to_all(mapped, "chan", 0, 0)
        else:
            (state,) = update(message, state, mixers[layer], None)
    return unpacked(lax.all_to_all(state, "chan", 0, 0), features.shape)


def solution(mesh):
    placed = (
        P(None, "space"),
        P("chan", "space"),
        P("space"),
        P(None, "space"),
        P(None, "chan", None),
        P(None, None, "chan"),
        P(None, None, "chan"),
    )
    return jax.shard_map(
        shards, mesh=mesh, in_specs=placed, out_specs=P("chan", "space"), check_vma=False
    )
```

```python
import functools
import math

import jax
import jax.numpy as jnp
from jax import lax
from jax.experimental import pallas as pl
from jax.experimental.pallas import tpu as pltpu
from jax.sharding import PartitionSpec as P

K = 8
LAYERS = 2
BLK = 128
LANES = 128

cutoff_radius = 6.0
gamma_width = 1.5
step_width = cutoff_radius / (K - 1)
MID = 4
FAR = 1000.0
SLOTS = 6
NEAR = 4

ENVELOPE = (
    0.02777777772845049,
    -0.00018032445737786967,
    4.2799604015759175e-07,
    -5.319790167613903e-10,
    3.90316047548473e-13,
)

VMEM = pltpu.MemorySpace.VMEM
SMEM = pltpu.MemorySpace.SMEM


def shifted(block, axis, distance):
    devices = range(lax.axis_size(axis))
    route = [((i - distance) % len(devices), i) for i in devices]
    return lax.ppermute(block, axis, route)


def split(value):
    high = value.astype(jnp.bfloat16)
    low = (value - high.astype(jnp.float32)).astype(jnp.bfloat16)
    return high, low


def basis_kernel(first_ref, second_ref, count_ref, rows_ref, columns_ref, out_ref, done_ref, wide, buf, sem):
    done_ref[0] = 1
    blocks = columns_ref.shape[0]
    for block in range(blocks):
        for axis in range(3):
            wide[block * 3 + axis] = jnp.broadcast_to(columns_ref[block, :, axis : axis + 1], (BLK, BLK))
    count = count_ref[0]
    chunk = 32

    def one(pair, carry):
        slot = lax.rem(pair, SLOTS)

        @pl.when(pair >= SLOTS)
        def _():
            pltpu.make_async_copy(buf.at[slot], out_ref.at[pair - SLOTS], sem.at[slot]).wait()

        first, second = first_ref[pair], second_ref[pair]
        same = (first == second).astype(jnp.float32)
        for part in range(BLK // chunk):
            rows = slice(part * chunk, (part + 1) * chunk)
            squared = None
            for axis in range(3):
                offset = wide[first * 3 + axis, rows, :] - rows_ref[second, axis : axis + 1, :]
                squared = offset * offset if squared is None else squared + offset * offset
            here = lax.broadcasted_iota(jnp.int32, (chunk, BLK), 0) + part * chunk
            there = lax.broadcasted_iota(jnp.int32, (chunk, BLK), 1)
            squared = squared + jnp.where(here == there, same * FAR, 0.0)
            squared = jnp.minimum(squared, cutoff_radius * cutoff_radius)
            distance = squared * lax.rsqrt(jnp.maximum(squared, 1e-20))
            bell = ENVELOPE[4]
            for power in (3, 2, 1, 0):
                bell = bell * squared + ENVELOPE[power]
            bell = bell * (cutoff_radius * cutoff_radius - squared)
            bell = bell * bell
            away = distance - MID * step_width
            middle = bell * jnp.exp(away * away * -gamma_width)
            up = jnp.exp(away * (2.0 * gamma_width * step_width))
            down = jnp.exp(away * (-2.0 * gamma_width * step_width))

            def keep(k, value):
                high, low = split(value)
                buf[slot, 0, k * BLK + part * chunk : k * BLK + (part + 1) * chunk, :] = high
                buf[slot, 1, k * BLK + part * chunk : k * BLK + (part + 1) * chunk, :] = low

            keep(MID, middle)
            value = middle
            for k in range(MID + 1, K):
                value = value * up
                keep(k, value)
            value = middle
            for k in range(MID - 1, -1, -1):
                value = value * down
                keep(k, value)
        pltpu.make_async_copy(buf.at[slot], out_ref.at[pair], sem.at[slot]).start()
        return carry

    lax.fori_loop(0, count, one, 0)

    for slot in range(SLOTS):

        @pl.when(slot < count)
        def _():
            pltpu.make_async_copy(buf.at[slot], out_ref.at[slot], sem.at[slot]).wait()


def bases(first, second, count, rows, columns):
    pairs = first.shape[0]
    blocks = columns.shape[0]
    return pl.pallas_call(
        basis_kernel,
        out_shape=[
            jax.ShapeDtypeStruct((pairs, 2, K * BLK, BLK), jnp.bfloat16),
            jax.ShapeDtypeStruct((1,), jnp.int32),
        ],
        in_specs=[pl.BlockSpec(memory_space=SMEM)] * 3 + [pl.BlockSpec(memory_space=VMEM)] * 2,
        out_specs=[pl.BlockSpec(memory_space=pl.ANY), pl.BlockSpec(memory_space=SMEM)],
        scratch_shapes=[
            pltpu.VMEM((blocks * 3, BLK, BLK), jnp.float32),
            pltpu.VMEM((SLOTS, 2, K * BLK, BLK), jnp.bfloat16),
            pltpu.SemaphoreType.DMA((SLOTS,)),
        ],
        cost_estimate=pl.CostEstimate(flops=pairs * K * BLK * BLK * 10, transcendentals=pairs * BLK * BLK * 4, bytes_accessed=pairs * K * BLK * BLK * 4),
        name="bases",
    )(first, second, count, rows, columns)


def unpack_block(even, odd):
    lane = lax.broadcasted_iota(jnp.int32, even.shape, 1)
    half = LANES // 2
    top = jnp.where(lane < half, even, pltpu.roll(odd, half, 1))
    bottom = jnp.where(lane < half, pltpu.roll(even, half, 1), odd)
    return jnp.concatenate([top, bottom], axis=0)


def pack_block(block):
    channels = block.shape[0]
    top, bottom = block[: channels // 2], block[channels // 2 :]
    lane = lax.broadcasted_iota(jnp.int32, top.shape, 1)
    half = LANES // 2
    even = jnp.where(lane < half, top, pltpu.roll(bottom, half, 1))
    odd = jnp.where(lane < half, pltpu.roll(top, half, 1), bottom)
    return even, odd


def pair_kernel(parts, blocks, *refs):
    first_ref, second_ref, range_ref, weight_ref = refs[:4]
    mapped = refs[4 : 4 + parts]
    basis_ref = refs[4 + parts]
    outs = refs[5 + parts : 5 + 2 * parts]
    scaled, total, buf, sem = refs[5 + 2 * parts :]
    channels = total.shape[1]
    start, stop = range_ref[0], range_ref[1]

    def fetch(pair, slot):
        return pltpu.make_async_copy(basis_ref.at[pair], buf.at[slot], sem.at[slot])

    for early in range(SLOTS):

        @pl.when(start + early < stop)
        def _():
            fetch(start + early, early).start()

    for part in range(parts):
        for block in range(blocks):
            total[part * blocks + block] = unpack_block(mapped[part][2 * block], mapped[part][2 * block + 1])

    def scale(block, carry):
        feature = total[block]
        for k in range(K):
            high, low = split(feature * weight_ref[k])
            scaled[block, :channels, k * BLK : (k + 1) * BLK] = high
            scaled[block, channels:, k * BLK : (k + 1) * BLK] = low
        total[block] = jnp.zeros_like(feature)
        return carry

    lax.fori_loop(0, parts * blocks, scale, 0)

    def fold(whole):
        return (whole[:channels, :BLK] + whole[:channels, BLK:]) + (whole[channels:, :BLK] + whole[channels:, BLK:])

    def products(pair, slot):
        first, second = first_ref[pair], second_ref[pair]
        across = jnp.concatenate([buf[slot, 0], buf[slot, 1]], axis=1)
        to_second = jnp.dot(scaled[first], across, preferred_element_type=jnp.float32)
        down = jnp.concatenate(
            [jnp.concatenate([buf[slot, h, k * BLK : (k + 1) * BLK, :] for k in range(K)], axis=1) for h in range(2)],
            axis=0,
        )
        to_first = lax.dot_general(
            scaled[second], down, (((1,), (1,)), ((), ())), preferred_element_type=jnp.float32
        )
        return first, second, fold(to_first), fold(to_second)

    def add(first, second, to_first, to_second, keep):
        differs = jnp.where(first != second, keep, 0.0)
        total[first] = total[first] + to_first * keep
        total[second] = total[second] + to_second * differs

    def two(turn, carry):
        pair = start + 2 * turn
        slot = lax.rem(2 * turn, SLOTS)
        more = pair + 1 < stop
        fetch(pair, slot).wait()

        @pl.when(more)
        def _():
            fetch(pair + 1, slot + 1).wait()

        one = products(pair, slot)
        other = products(jnp.where(more, pair + 1, pair), jnp.where(more, slot + 1, slot))
        add(*one, 1.0)
        add(*other, jnp.where(more, 1.0, 0.0))
        for ahead in range(2):

            @pl.when(pair + SLOTS + ahead < stop)
            def _():
                fetch(pair + SLOTS + ahead, slot + ahead).start()

        return carry

    lax.fori_loop(0, (stop - start + 1) // 2, two, 0)
    for part in range(parts):
        for block in range(blocks):
            even, odd = pack_block(total[part * blocks + block])
            outs[part][2 * block] = even
            outs[part][2 * block + 1] = odd


def pair_messages(first, second, span, weights, mapped, basis, blocks):
    parts = len(mapped)
    channels = weights.shape[1]
    piece = mapped[0].shape
    return pl.pallas_call(
        functools.partial(pair_kernel, parts, blocks),
        out_shape=[jax.ShapeDtypeStruct(piece, jnp.float32)] * parts,
        in_specs=[pl.BlockSpec(memory_space=SMEM)] * 3
        + [pl.BlockSpec(memory_space=VMEM)] * (1 + parts)
        + [pl.BlockSpec(memory_space=pl.ANY)],
        out_specs=[pl.BlockSpec(memory_space=VMEM)] * parts,
        scratch_shapes=[
            pltpu.VMEM((parts * blocks, 2 * channels, K * BLK), jnp.bfloat16),
            pltpu.VMEM((parts * blocks, channels, BLK), jnp.float32),
            pltpu.VMEM((SLOTS, 2, K * BLK, BLK), jnp.bfloat16),
            pltpu.SemaphoreType.DMA((SLOTS,)),
        ],
        cost_estimate=pl.CostEstimate(flops=parts * 8 * K * BLK * BLK * channels * 16, transcendentals=0, bytes_accessed=parts * 8 * K * BLK * BLK * 4),
        name="pairs",
    )(first, second, span, weights, *mapped, basis)


def sum_kernel(*refs):
    total = refs[0][...]
    for ref in refs[1:-1]:
        total = total + ref[...]
    refs[-1][...] = total


def summed(pieces):
    return pl.pallas_call(
        sum_kernel,
        out_shape=jax.ShapeDtypeStruct(pieces[0].shape, jnp.float32),
        in_specs=[pl.BlockSpec(memory_space=VMEM)] * len(pieces),
        out_specs=pl.BlockSpec(memory_space=VMEM),
        name="summed",
    )(*pieces)


def first_map_kernel(weight_ref, state_ref, after_ref, out_ref):
    product = jnp.dot(
        weight_ref[...], state_ref[...], precision=lax.Precision.HIGHEST, preferred_element_type=jnp.float32
    )
    for block in range(state_ref.shape[1] // BLK):
        even, odd = pack_block(product[:, block * BLK : (block + 1) * BLK])
        out_ref[2 * block] = even
        out_ref[2 * block + 1] = odd


def first_map(weight, state, after):
    channels = weight.shape[0]
    return pl.pallas_call(
        first_map_kernel,
        out_shape=jax.ShapeDtypeStruct((state.shape[1] // 64, channels // 2, LANES), jnp.float32),
        in_specs=[pl.BlockSpec(memory_space=VMEM)] * 2 + [pl.BlockSpec(memory_space=SMEM)],
        out_specs=pl.BlockSpec(memory_space=VMEM),
        name="first_map",
    )(weight, state, after)


def packed_product(weight_ref, value):
    groups = value.shape[0]
    turned = [pltpu.roll(value[g], LANES // 2, 1) for g in range(groups)]
    lower = jnp.concatenate([x for g in range(groups) for x in (value[g], turned[g])], axis=0)
    upper = jnp.concatenate([x for g in range(groups) for x in (turned[g], value[g])], axis=0)
    left = jnp.dot(weight_ref[0], lower, precision=lax.Precision.HIGHEST, preferred_element_type=jnp.float32)
    right = jnp.dot(weight_ref[1], upper, precision=lax.Precision.HIGHEST, preferred_element_type=jnp.float32)
    lane = lax.broadcasted_iota(jnp.int32, left.shape, 1)
    return jnp.where(lane < LANES // 2, left, right).reshape(value.shape)


def update_kernel(last, message_ref, state_ref, mix_ref, *rest):
    mixed = packed_product(mix_ref, message_ref[...])
    state = state_ref[...] + mixed / (1.0 + jnp.exp(-mixed))
    if last:
        rest[0][...] = state
    else:
        map_ref, state_out, mapped_out = rest
        state_out[...] = state
        mapped_out[...] = packed_product(map_ref, state)


def update(message, state, mix, map_next):
    last = map_next is None
    shape = jax.ShapeDtypeStruct(message.shape, jnp.float32)
    operands = (message, state, mix) + (() if last else (map_next,))
    return pl.pallas_call(
        functools.partial(update_kernel, last),
        out_shape=[shape] if last else [shape, shape],
        in_specs=[pl.BlockSpec(memory_space=VMEM)] * len(operands),
        out_specs=[pl.BlockSpec(memory_space=VMEM)] * (1 if last else 2),
        name="update",
    )(*operands)


def unpack_kernel(value_ref, out_ref):
    for block in range(out_ref.shape[1] // BLK):
        out_ref[:, block * BLK : (block + 1) * BLK] = unpack_block(value_ref[2 * block], value_ref[2 * block + 1])


def unpacked(value, shape):
    return pl.pallas_call(
        unpack_kernel,
        out_shape=jax.ShapeDtypeStruct(shape, jnp.float32),
        in_specs=[pl.BlockSpec(memory_space=VMEM)],
        out_specs=pl.BlockSpec(memory_space=VMEM),
        name="unpacked",
    )(value)


def half_rows(weight):
    return weight.reshape(-1, 2, 32, weight.shape[1]).transpose(1, 0, 2, 3).reshape(2, -1, weight.shape[1])


def shards(positions, features, block_counts, pair_table, in_weight, filter_weight, mix_weight):
    spatial = lax.axis_size("space")
    reach_dev = spatial // 4
    own_index = lax.axis_index("space")
    own_chan = lax.axis_index("chan")
    blocks = block_counts.shape[0]
    atoms_dev = positions.shape[1]
    gathered = lax.all_gather(features, "chan", axis=0, tiled=True)

    valid = (lax.broadcasted_iota(jnp.int32, (blocks, BLK), 1) < block_counts[:, None]).reshape(1, atoms_dev)
    geometry = jnp.concatenate([positions, valid.astype(jnp.float32)], axis=0)[None]
    last = shifted(geometry, "space", -reach_dev)
    everywhere, reached = geometry, 1
    while reached < reach_dev:
        everywhere = jnp.concatenate([everywhere, shifted(everywhere, "space", -reached)], axis=0)
        reached = 2 * reached
    everywhere = jnp.concatenate([everywhere[:reach_dev], last], axis=0)
    there = jnp.concatenate(
        [jnp.where(everywhere[:, 3:4] > 0.5, everywhere[:, :1], -FAR), everywhere[:, 1:]], axis=1
    )
    rows = there.reshape(reach_dev + 1, 4, blocks, BLK).transpose(0, 2, 1, 3).reshape(-1, 4, BLK)
    here = jnp.concatenate([jnp.where(valid, positions[:1], FAR), geometry[0, 1:]], axis=0)
    columns = here.reshape(4, blocks, BLK).transpose(1, 2, 0)

    pairs = pair_table.shape[1]
    ahead = (pair_table[1] // blocks - own_index) % spatial
    live = pair_table[2] > 0
    early, late = live & (ahead <= NEAR), live & (ahead > NEAR)
    before = lax.broadcasted_iota(jnp.int32, (pairs, pairs), 0) < lax.broadcasted_iota(jnp.int32, (pairs, pairs), 1)
    early_count = jnp.sum(early.astype(jnp.int32))
    count = early_count + jnp.sum(late.astype(jnp.int32))
    early_rank = jnp.sum((before & early[:, None]).astype(jnp.int32), axis=0)
    late_rank = jnp.sum((before & late[:, None]).astype(jnp.int32), axis=0) + early_count
    rank = jnp.where(early, early_rank, jnp.where(late, late_rank, pairs))
    chosen = rank[:, None] == lax.broadcasted_iota(jnp.int32, (pairs, pairs), 1)
    packed = (ahead * blocks + pair_table[1] % blocks) * blocks + (pair_table[0] - own_index * blocks)
    packed = jnp.sum(jnp.where(chosen, packed[:, None], 0), axis=0)
    first, second = packed % blocks, packed // blocks
    slots = [list(range(NEAR + 1)), [0] + list(range(NEAR + 1, reach_dev + 1))]
    seconds = [second, second - NEAR * blocks]
    spans = [
        jnp.stack([jnp.zeros_like(count), early_count]),
        jnp.stack([early_count, count]),
    ]
    basis, after = bases(first, second, count.reshape(1), rows, columns)

    centre = (jnp.arange(K, dtype=jnp.float32) - MID) * step_width
    damp = jnp.exp(-gamma_width * centre * centre)
    weights = jnp.broadcast_to(
        (filter_weight * damp[None, :, None])[..., None], filter_weight.shape + (BLK,)
    )

    mapped = first_map(in_weight[0], gathered, after)
    own_atoms = lax.dynamic_slice_in_dim(gathered, own_chan * 64, 64, 1)
    state = own_atoms.reshape(-1, 2, 32, 64).transpose(0, 2, 1, 3).reshape(-1, 32, LANES)
    mixers = [
        half_rows(lax.all_gather(mix_weight[layer].T, "chan", axis=0, tiled=True).T) for layer in range(LAYERS)
    ]
    mappers = [None] + [
        half_rows(lax.all_gather(in_weight[layer], "chan", axis=0, tiled=True)) for layer in range(1, LAYERS)
    ]
    for layer in range(LAYERS):
        near = [mapped]
        for offset in range(1, reach_dev + 1):
            near.append(shifted(mapped, "space", -offset))
        pieces, returned = [], []
        for part in range(2):
            sent = pair_messages(
                first, seconds[part], spans[part], weights[layer], [near[i] for i in slots[part]], basis, blocks
            )
            pieces.append(sent[0])
            returned += [shifted(x, "space", i) for x, i in zip(sent[1:], slots[part][1:])]
        received = summed(pieces + returned)
        message = lax.all_to_all(received, "chan", 0, 0)
        if layer + 1 < LAYERS:
            state, mapped = update(message, state, mixers[layer], mappers[layer + 1])
            mapped = lax.all_to_all(mapped, "chan", 0, 0)
        else:
            (state,) = update(message, state, mixers[layer], None)
    return unpacked(lax.all_to_all(state, "chan", 0, 0), features.shape)


def solution(mesh):
    placed = (
        P(None, "space"),
        P("chan", "space"),
        P("space"),
        P(None, "space"),
        P(None, "chan", None),
        P(None, None, "chan"),
        P(None, None, "chan"),
    )
    return jax.shard_map(
        shards, mesh=mesh, in_specs=placed, out_specs=P("chan", "space"), check_vma=False
    )
```

```python
import functools
import math

import jax
import jax.numpy as jnp
from jax import lax
from jax.experimental import pallas as pl
from jax.experimental.pallas import tpu as pltpu
from jax.sharding import PartitionSpec as P

K = 8
LAYERS = 2
BLK = 128
LANES = 128

cutoff_radius = 6.0
gamma_width = 1.5
step_width = cutoff_radius / (K - 1)
MID = 4
FAR = 1000.0
SLOTS = 6
NEAR = 4

ENVELOPE = (
    0.02777777772845049,
    -0.00018032445737786967,
    4.2799604015759175e-07,
    -5.319790167613903e-10,
    3.90316047548473e-13,
)

VMEM = pltpu.MemorySpace.VMEM
SMEM = pltpu.MemorySpace.SMEM


def shifted(block, axis, distance):
    devices = range(lax.axis_size(axis))
    route = [((i - distance) % len(devices), i) for i in devices]
    return lax.ppermute(block, axis, route)


def split(value):
    high = value.astype(jnp.bfloat16)
    low = (value - high.astype(jnp.float32)).astype(jnp.bfloat16)
    return high, low


def basis_kernel(first_ref, second_ref, count_ref, rows_ref, columns_ref, out_ref, done_ref, wide, buf, sem):
    done_ref[0] = 1
    blocks = columns_ref.shape[0]
    for block in range(blocks):
        for axis in range(3):
            wide[block * 3 + axis] = jnp.broadcast_to(columns_ref[block, :, axis : axis + 1], (BLK, BLK))
    count = count_ref[0]
    chunk = 32

    def one(pair, carry):
        slot = lax.rem(pair, SLOTS)

        @pl.when(pair >= SLOTS)
        def _():
            pltpu.make_async_copy(buf.at[slot], out_ref.at[pair - SLOTS], sem.at[slot]).wait()

        first, second = first_ref[pair], second_ref[pair]
        same = (first == second).astype(jnp.float32)
        for part in range(BLK // chunk):
            rows = slice(part * chunk, (part + 1) * chunk)
            squared = None
            for axis in range(3):
                offset = wide[first * 3 + axis, rows, :] - rows_ref[second, axis : axis + 1, :]
                squared = offset * offset if squared is None else squared + offset * offset
            here = lax.broadcasted_iota(jnp.int32, (chunk, BLK), 0) + part * chunk
            there = lax.broadcasted_iota(jnp.int32, (chunk, BLK), 1)
            squared = squared + jnp.where(here == there, same * FAR, 0.0)
            squared = jnp.minimum(squared, cutoff_radius * cutoff_radius)
            distance = squared * lax.rsqrt(jnp.maximum(squared, 1e-20))
            bell = ENVELOPE[4]
            for power in (3, 2, 1, 0):
                bell = bell * squared + ENVELOPE[power]
            bell = bell * (cutoff_radius * cutoff_radius - squared)
            bell = bell * bell
            away = distance - MID * step_width
            middle = bell * jnp.exp(away * away * -gamma_width)
            up = jnp.exp(away * (2.0 * gamma_width * step_width))
            down = jnp.exp(away * (-2.0 * gamma_width * step_width))

            def keep(k, value):
                high, low = split(value)
                buf[slot, 0, k * BLK + part * chunk : k * BLK + (part + 1) * chunk, :] = high
                buf[slot, 1, k * BLK + part * chunk : k * BLK + (part + 1) * chunk, :] = low

            keep(MID, middle)
            value = middle
            for k in range(MID + 1, K):
                value = value * up
                keep(k, value)
            value = middle
            for k in range(MID - 1, -1, -1):
                value = value * down
                keep(k, value)
        pltpu.make_async_copy(buf.at[slot], out_ref.at[pair], sem.at[slot]).start()
        return carry

    lax.fori_loop(0, count, one, 0)

    for slot in range(SLOTS):

        @pl.when(slot < count)
        def _():
            pltpu.make_async_copy(buf.at[slot], out_ref.at[slot], sem.at[slot]).wait()


def bases(first, second, count, rows, columns):
    pairs = first.shape[0]
    blocks = columns.shape[0]
    return pl.pallas_call(
        basis_kernel,
        out_shape=[
            jax.ShapeDtypeStruct((pairs, 2, K * BLK, BLK), jnp.bfloat16),
            jax.ShapeDtypeStruct((1,), jnp.int32),
        ],
        in_specs=[pl.BlockSpec(memory_space=SMEM)] * 3 + [pl.BlockSpec(memory_space=VMEM)] * 2,
        out_specs=[pl.BlockSpec(memory_space=pl.ANY), pl.BlockSpec(memory_space=SMEM)],
        scratch_shapes=[
            pltpu.VMEM((blocks * 3, BLK, BLK), jnp.float32),
            pltpu.VMEM((SLOTS, 2, K * BLK, BLK), jnp.bfloat16),
            pltpu.SemaphoreType.DMA((SLOTS,)),
        ],
        cost_estimate=pl.CostEstimate(flops=pairs * K * BLK * BLK * 10, transcendentals=pairs * BLK * BLK * 4, bytes_accessed=pairs * K * BLK * BLK * 4),
        name="bases",
    )(first, second, count, rows, columns)


def unpack_block(even, odd):
    lane = lax.broadcasted_iota(jnp.int32, even.shape, 1)
    half = LANES // 2
    top = jnp.where(lane < half, even, pltpu.roll(odd, half, 1))
    bottom = jnp.where(lane < half, pltpu.roll(even, half, 1), odd)
    return jnp.concatenate([top, bottom], axis=0)


def pack_block(block):
    channels = block.shape[0]
    top, bottom = block[: channels // 2], block[channels // 2 :]
    lane = lax.broadcasted_iota(jnp.int32, top.shape, 1)
    half = LANES // 2
    even = jnp.where(lane < half, top, pltpu.roll(bottom, half, 1))
    odd = jnp.where(lane < half, pltpu.roll(top, half, 1), bottom)
    return even, odd


def pair_kernel(far, parts, blocks, *refs):
    first_ref, second_ref, count_ref, weight_ref = refs[:4]
    mapped = refs[4 : 4 + parts]
    basis_ref = refs[4 + parts]
    outs = refs[5 + parts : 5 + 2 * parts]
    wide, scaled, total, buf, sem = refs[5 + 2 * parts :]
    channels = total.shape[1]
    start, stop = (count_ref[0], count_ref[1]) if far else (0, count_ref[0])

    def fetch(pair, slot):
        return pltpu.make_async_copy(basis_ref.at[pair], buf.at[slot], sem.at[slot])

    for early in range(SLOTS):

        @pl.when(start + early < stop)
        def _():
            fetch(start + early, early).start()

    for k in range(K):
        wide[k] = jnp.broadcast_to(weight_ref[:, k : k + 1], wide.shape[1:])
    for part in range(parts):
        for block in range(blocks):
            total[part * blocks + block] = unpack_block(mapped[part][2 * block], mapped[part][2 * block + 1])

    def scale(block, carry):
        feature = total[block]
        for k in range(K):
            high, low = split(feature * wide[k])
            scaled[block, :channels, k * BLK : (k + 1) * BLK] = high
            scaled[block, channels:, k * BLK : (k + 1) * BLK] = low
        total[block] = jnp.zeros_like(feature)
        return carry

    lax.fori_loop(0, parts * blocks, scale, 0)

    def fold(whole):
        return (whole[:channels, :BLK] + whole[:channels, BLK:]) + (whole[channels:, :BLK] + whole[channels:, BLK:])

    def products(pair, slot):
        first, second = first_ref[pair], second_ref[pair] - (NEAR * blocks if far else 0)
        across = jnp.concatenate([buf[slot, 0], buf[slot, 1]], axis=1)
        to_second = jnp.dot(scaled[first], across, preferred_element_type=jnp.float32)
        down = jnp.concatenate(
            [jnp.concatenate([buf[slot, h, k * BLK : (k + 1) * BLK, :] for k in range(K)], axis=1) for h in range(2)],
            axis=0,
        )
        to_first = lax.dot_general(
            scaled[second], down, (((1,), (1,)), ((), ())), preferred_element_type=jnp.float32
        )
        return first, second, fold(to_first), fold(to_second)

    def add(first, second, to_first, to_second, keep):
        differs = jnp.where(first != second, keep, 0.0)
        total[first] = total[first] + to_first * keep
        total[second] = total[second] + to_second * differs

    def two(turn, carry):
        pair = start + 2 * turn
        slot = lax.rem(2 * turn, SLOTS)
        more = pair + 1 < stop
        fetch(pair, slot).wait()

        @pl.when(more)
        def _():
            fetch(pair + 1, slot + 1).wait()

        one = products(pair, slot)
        other = products(jnp.where(more, pair + 1, pair), jnp.where(more, slot + 1, slot))
        add(*one, 1.0)
        add(*other, jnp.where(more, 1.0, 0.0))
        for ahead in range(2):

            @pl.when(pair + SLOTS + ahead < stop)
            def _():
                fetch(pair + SLOTS + ahead, slot + ahead).start()

        return carry

    lax.fori_loop(0, (stop - start + 1) // 2, two, 0)
    for part in range(parts):
        for block in range(blocks):
            even, odd = pack_block(total[part * blocks + block])
            outs[part][2 * block] = even
            outs[part][2 * block + 1] = odd


def pair_messages(far, first, second, span, weights, mapped, basis, blocks):
    parts = len(mapped)
    channels = weights.shape[0]
    piece = mapped[0].shape
    return pl.pallas_call(
        functools.partial(pair_kernel, far, parts, blocks),
        out_shape=[jax.ShapeDtypeStruct(piece, jnp.float32)] * parts,
        in_specs=[pl.BlockSpec(memory_space=SMEM)] * 3
        + [pl.BlockSpec(memory_space=VMEM)] * (1 + parts)
        + [pl.BlockSpec(memory_space=pl.ANY)],
        out_specs=[pl.BlockSpec(memory_space=VMEM)] * parts,
        scratch_shapes=[
            pltpu.VMEM((K, channels, BLK), jnp.float32),
            pltpu.VMEM((parts * blocks, 2 * channels, K * BLK), jnp.bfloat16),
            pltpu.VMEM((parts * blocks, channels, BLK), jnp.float32),
            pltpu.VMEM((SLOTS, 2, K * BLK, BLK), jnp.bfloat16),
            pltpu.SemaphoreType.DMA((SLOTS,)),
        ],
        cost_estimate=pl.CostEstimate(flops=parts * 8 * K * BLK * BLK * channels * 16, transcendentals=0, bytes_accessed=parts * 8 * K * BLK * BLK * 4),
        name="pairs",
    )(first, second, span, weights, *mapped, basis)


def sum_kernel(*refs):
    total = refs[0][...]
    for ref in refs[1:-1]:
        total = total + ref[...]
    refs[-1][...] = total


def summed(pieces):
    return pl.pallas_call(
        sum_kernel,
        out_shape=jax.ShapeDtypeStruct(pieces[0].shape, jnp.float32),
        in_specs=[pl.BlockSpec(memory_space=VMEM)] * len(pieces),
        out_specs=pl.BlockSpec(memory_space=VMEM),
        name="summed",
    )(*pieces)


def first_map_kernel(weight_ref, state_ref, after_ref, out_ref):
    product = jnp.dot(
        weight_ref[...], state_ref[...], precision=lax.Precision.HIGHEST, preferred_element_type=jnp.float32
    )
    for block in range(state_ref.shape[1] // BLK):
        even, odd = pack_block(product[:, block * BLK : (block + 1) * BLK])
        out_ref[2 * block] = even
        out_ref[2 * block + 1] = odd


def first_map(weight, state, after):
    channels = weight.shape[0]
    return pl.pallas_call(
        first_map_kernel,
        out_shape=jax.ShapeDtypeStruct((state.shape[1] // 64, channels // 2, LANES), jnp.float32),
        in_specs=[pl.BlockSpec(memory_space=VMEM)] * 2 + [pl.BlockSpec(memory_space=SMEM)],
        out_specs=pl.BlockSpec(memory_space=VMEM),
        name="first_map",
    )(weight, state, after)


def packed_product(weight_ref, value):
    groups = value.shape[0]
    turned = [pltpu.roll(value[g], LANES // 2, 1) for g in range(groups)]
    lower = jnp.concatenate([x for g in range(groups) for x in (value[g], turned[g])], axis=0)
    upper = jnp.concatenate([x for g in range(groups) for x in (turned[g], value[g])], axis=0)
    left = jnp.dot(weight_ref[0], lower, precision=lax.Precision.HIGHEST, preferred_element_type=jnp.float32)
    right = jnp.dot(weight_ref[1], upper, precision=lax.Precision.HIGHEST, preferred_element_type=jnp.float32)
    lane = lax.broadcasted_iota(jnp.int32, left.shape, 1)
    return jnp.where(lane < LANES // 2, left, right).reshape(value.shape)


def update_kernel(message_ref, state_ref, mix_ref, map_ref, final_ref, state_out, sending_out):
    mixed = packed_product(mix_ref, message_ref[...])
    state = state_ref[...] + mixed / (1.0 + jnp.exp(-mixed))
    state_out[...] = state
    sending_out[...] = state

    @pl.when(final_ref[0] == 0)
    def _():
        sending_out[...] = packed_product(map_ref, state)


def update(message, state, mix, map_next, final):
    shape = jax.ShapeDtypeStruct(message.shape, jnp.float32)
    return pl.pallas_call(
        update_kernel,
        out_shape=[shape, shape],
        in_specs=[pl.BlockSpec(memory_space=VMEM)] * 4 + [pl.BlockSpec(memory_space=SMEM)],
        out_specs=[pl.BlockSpec(memory_space=VMEM)] * 2,
        name="update",
    )(message, state, mix, map_next, final)


def unpack_kernel(value_ref, out_ref):
    for block in range(out_ref.shape[1] // BLK):
        out_ref[:, block * BLK : (block + 1) * BLK] = unpack_block(value_ref[2 * block], value_ref[2 * block + 1])


def unpacked(value, shape):
    return pl.pallas_call(
        unpack_kernel,
        out_shape=jax.ShapeDtypeStruct(shape, jnp.float32),
        in_specs=[pl.BlockSpec(memory_space=VMEM)],
        out_specs=pl.BlockSpec(memory_space=VMEM),
        name="unpacked",
    )(value)


def half_rows(weight):
    return weight.reshape(-1, 2, 32, weight.shape[1]).transpose(1, 0, 2, 3).reshape(2, -1, weight.shape[1])


def shards(positions, features, block_counts, pair_table, in_weight, filter_weight, mix_weight):
    spatial = lax.axis_size("space")
    reach_dev = spatial // 4
    own_index = lax.axis_index("space")
    own_chan = lax.axis_index("chan")
    blocks = block_counts.shape[0]
    atoms_dev = positions.shape[1]
    gathered = lax.all_gather(features, "chan", axis=0, tiled=True)

    valid = (lax.broadcasted_iota(jnp.int32, (blocks, BLK), 1) < block_counts[:, None]).reshape(1, atoms_dev)
    geometry = jnp.concatenate([positions, valid.astype(jnp.float32)], axis=0)[None]
    last = shifted(geometry, "space", -reach_dev)
    everywhere, reached = geometry, 1
    while reached < reach_dev:
        everywhere = jnp.concatenate([everywhere, shifted(everywhere, "space", -reached)], axis=0)
        reached = 2 * reached
    everywhere = jnp.concatenate([everywhere[:reach_dev], last], axis=0)
    there = jnp.concatenate(
        [jnp.where(everywhere[:, 3:4] > 0.5, everywhere[:, :1], -FAR), everywhere[:, 1:]], axis=1
    )
    rows = there.reshape(reach_dev + 1, 4, blocks, BLK).transpose(0, 2, 1, 3).reshape(-1, 4, BLK)
    here = jnp.concatenate([jnp.where(valid, positions[:1], FAR), geometry[0, 1:]], axis=0)
    columns = here.reshape(4, blocks, BLK).transpose(1, 2, 0)

    pairs = pair_table.shape[1]
    ahead = (pair_table[1] // blocks - own_index) % spatial
    live = pair_table[2] > 0
    early, late = live & (ahead <= NEAR), live & (ahead > NEAR)
    before = lax.broadcasted_iota(jnp.int32, (pairs, pairs), 0) < lax.broadcasted_iota(jnp.int32, (pairs, pairs), 1)
    early_count = jnp.sum(early.astype(jnp.int32))
    count = early_count + jnp.sum(late.astype(jnp.int32))
    early_rank = jnp.sum((before & early[:, None]).astype(jnp.int32), axis=0)
    late_rank = jnp.sum((before & late[:, None]).astype(jnp.int32), axis=0) + early_count
    rank = jnp.where(early, early_rank, jnp.where(late, late_rank, pairs))
    chosen = rank[:, None] == lax.broadcasted_iota(jnp.int32, (pairs, pairs), 1)
    packed = (ahead * blocks + pair_table[1] % blocks) * blocks + (pair_table[0] - own_index * blocks)
    packed = jnp.sum(jnp.where(chosen, packed[:, None], 0), axis=0)
    first, second = packed % blocks, packed // blocks
    slots = [list(range(NEAR + 1)), [0] + list(range(NEAR + 1, reach_dev + 1))]
    counts = jnp.stack([early_count, count])
    basis, after = bases(first, second, count.reshape(1), rows, columns)

    centre = (jnp.arange(K, dtype=jnp.float32) - MID) * step_width
    damp = jnp.exp(-gamma_width * centre * centre)
    weights = (filter_weight * damp[None, :, None]).transpose(0, 2, 1)

    mapped = first_map(in_weight[0], gathered, after)
    own_atoms = lax.dynamic_slice_in_dim(gathered, own_chan * 64, 64, 1)
    state = own_atoms.reshape(-1, 2, 32, 64).transpose(0, 2, 1, 3).reshape(-1, 32, LANES)
    mix_turned = mix_weight.transpose(0, 2, 1)

    def layer_turn(layer, carry):
        state, mapped = carry
        following = lax.rem(layer + 1, LAYERS)
        mix = half_rows(lax.all_gather(mix_turned[layer], "chan", axis=0, tiled=True).T)
        map_next = half_rows(lax.all_gather(in_weight[following], "chan", axis=0, tiled=True))
        near = [mapped]
        for offset in range(1, reach_dev + 1):
            near.append(shifted(mapped, "space", -offset))
        pieces, returned = [], []
        for far in range(2):
            sent = pair_messages(
                far, first, second, counts, weights[layer], [near[i] for i in slots[far]], basis, blocks
            )
            pieces.append(sent[0])
            returned += [shifted(x, "space", i) for x, i in zip(sent[1:], slots[far][1:])]
        received = summed(pieces + returned)
        message = lax.all_to_all(received, "chan", 0, 0)
        final = jnp.asarray(layer + 1 == LAYERS).astype(jnp.int32).reshape(1)
        state, sending = update(message, state, mix, map_next, final)
        return state, lax.all_to_all(sending, "chan", 0, 0)

    state, mapped = lax.fori_loop(0, LAYERS, layer_turn, (state, mapped))
    return unpacked(mapped, features.shape)


def solution(mesh):
    placed = (
        P(None, "space"),
        P("chan", "space"),
        P("space"),
        P(None, "space"),
        P(None, "chan", None),
        P(None, None, "chan"),
        P(None, None, "chan"),
    )
    return jax.shard_map(
        shards, mesh=mesh, in_specs=placed, out_specs=P("chan", "space"), check_vma=False
    )
```

```python
import functools
import math

import jax
import jax.numpy as jnp
from jax import lax
from jax.experimental import pallas as pl
from jax.experimental.pallas import tpu as pltpu
from jax.sharding import PartitionSpec as P

K = 8
LAYERS = 2
BLK = 128
LANES = 128

cutoff_radius = 6.0
gamma_width = 1.5
step_width = cutoff_radius / (K - 1)
MID = 4
FAR = 1000.0
SLOTS = 6
NEAR = 4

ENVELOPE = (
    0.02777777772845049,
    -0.00018032445737786967,
    4.2799604015759175e-07,
    -5.319790167613903e-10,
    3.90316047548473e-13,
)

VMEM = pltpu.MemorySpace.VMEM
SMEM = pltpu.MemorySpace.SMEM


def shifted(block, axis, distance):
    devices = range(lax.axis_size(axis))
    route = [((i - distance) % len(devices), i) for i in devices]
    return lax.ppermute(block, axis, route)


def along(block, target):
    return lax.ppermute(block, "space", [(i, target(i)) for i in range(lax.axis_size("space"))])


def split(value):
    high = value.astype(jnp.bfloat16)
    low = (value - high.astype(jnp.float32)).astype(jnp.bfloat16)
    return high, low


def basis_kernel(first_ref, second_ref, count_ref, rows_ref, columns_ref, out_ref, done_ref, wide, buf, sem):
    done_ref[0] = 1
    blocks = columns_ref.shape[0]
    for block in range(blocks):
        for axis in range(3):
            wide[block * 3 + axis] = jnp.broadcast_to(columns_ref[block, :, axis : axis + 1], (BLK, BLK))
    count = count_ref[0]
    chunk = 32

    def one(pair, carry):
        slot = lax.rem(pair, SLOTS)

        @pl.when(pair >= SLOTS)
        def _():
            pltpu.make_async_copy(buf.at[slot], out_ref.at[pair - SLOTS], sem.at[slot]).wait()

        first, second = first_ref[pair], second_ref[pair]
        same = (first == second).astype(jnp.float32)
        for part in range(BLK // chunk):
            rows = slice(part * chunk, (part + 1) * chunk)
            squared = None
            for axis in range(3):
                offset = wide[first * 3 + axis, rows, :] - rows_ref[second, axis : axis + 1, :]
                squared = offset * offset if squared is None else squared + offset * offset
            here = lax.broadcasted_iota(jnp.int32, (chunk, BLK), 0) + part * chunk
            there = lax.broadcasted_iota(jnp.int32, (chunk, BLK), 1)
            squared = squared + jnp.where(here == there, same * FAR, 0.0)
            squared = jnp.minimum(squared, cutoff_radius * cutoff_radius)
            distance = squared * lax.rsqrt(jnp.maximum(squared, 1e-20))
            bell = ENVELOPE[4]
            for power in (3, 2, 1, 0):
                bell = bell * squared + ENVELOPE[power]
            bell = bell * (cutoff_radius * cutoff_radius - squared)
            bell = bell * bell
            away = distance - MID * step_width
            middle = bell * jnp.exp(away * away * -gamma_width)
            up = jnp.exp(away * (2.0 * gamma_width * step_width))
            down = jnp.exp(away * (-2.0 * gamma_width * step_width))

            def keep(k, value):
                high, low = split(value)
                buf[slot, 0, k * BLK + part * chunk : k * BLK + (part + 1) * chunk, :] = high
                buf[slot, 1, k * BLK + part * chunk : k * BLK + (part + 1) * chunk, :] = low

            keep(MID, middle)
            value = middle
            for k in range(MID + 1, K):
                value = value * up
                keep(k, value)
            value = middle
            for k in range(MID - 1, -1, -1):
                value = value * down
                keep(k, value)
        pltpu.make_async_copy(buf.at[slot], out_ref.at[pair], sem.at[slot]).start()
        return carry

    lax.fori_loop(0, count, one, 0)

    for slot in range(SLOTS):

        @pl.when(slot < count)
        def _():
            pltpu.make_async_copy(buf.at[slot], out_ref.at[slot], sem.at[slot]).wait()


def bases(first, second, count, rows, columns):
    pairs = first.shape[0]
    blocks = columns.shape[0]
    return pl.pallas_call(
        basis_kernel,
        out_shape=[
            jax.ShapeDtypeStruct((pairs, 2, K * BLK, BLK), jnp.bfloat16),
            jax.ShapeDtypeStruct((1,), jnp.int32),
        ],
        in_specs=[pl.BlockSpec(memory_space=SMEM)] * 3 + [pl.BlockSpec(memory_space=VMEM)] * 2,
        out_specs=[pl.BlockSpec(memory_space=pl.ANY), pl.BlockSpec(memory_space=SMEM)],
        scratch_shapes=[
            pltpu.VMEM((blocks * 3, BLK, BLK), jnp.float32),
            pltpu.VMEM((SLOTS, 2, K * BLK, BLK), jnp.bfloat16),
            pltpu.SemaphoreType.DMA((SLOTS,)),
        ],
        cost_estimate=pl.CostEstimate(flops=pairs * K * BLK * BLK * 10, transcendentals=pairs * BLK * BLK * 4, bytes_accessed=pairs * K * BLK * BLK * 4),
        name="bases",
    )(first, second, count, rows, columns)


def unpack_block(even, odd):
    lane = lax.broadcasted_iota(jnp.int32, even.shape, 1)
    half = LANES // 2
    top = jnp.where(lane < half, even, pltpu.roll(odd, half, 1))
    bottom = jnp.where(lane < half, pltpu.roll(even, half, 1), odd)
    return jnp.concatenate([top, bottom], axis=0)


def pack_block(block):
    channels = block.shape[0]
    top, bottom = block[: channels // 2], block[channels // 2 :]
    lane = lax.broadcasted_iota(jnp.int32, top.shape, 1)
    half = LANES // 2
    even = jnp.where(lane < half, top, pltpu.roll(bottom, half, 1))
    odd = jnp.where(lane < half, pltpu.roll(top, half, 1), bottom)
    return even, odd


def pair_kernel(far, parts, blocks, *refs):
    first_ref, second_ref, count_ref, weight_ref = refs[:4]
    mapped = refs[4 : 4 + parts]
    basis_ref = refs[4 + parts]
    outs = refs[5 + parts : 5 + 2 * parts]
    wide, scaled, total, buf, sem = refs[5 + 2 * parts :]
    channels = total.shape[1]
    start, stop = (count_ref[0], count_ref[1]) if far else (0, count_ref[0])

    def fetch(pair, slot):
        return pltpu.make_async_copy(basis_ref.at[pair], buf.at[slot], sem.at[slot])

    for early in range(SLOTS):

        @pl.when(start + early < stop)
        def _():
            fetch(start + early, early).start()

    for k in range(K):
        wide[k] = jnp.broadcast_to(weight_ref[:, k : k + 1], wide.shape[1:])
    for part in range(parts):
        for block in range(blocks):
            total[part * blocks + block] = unpack_block(mapped[part][2 * block], mapped[part][2 * block + 1])

    def scale(block, carry):
        feature = total[block]
        for k in range(K):
            high, low = split(feature * wide[k])
            scaled[block, :channels, k * BLK : (k + 1) * BLK] = high
            scaled[block, channels:, k * BLK : (k + 1) * BLK] = low
        total[block] = jnp.zeros_like(feature)
        return carry

    lax.fori_loop(0, parts * blocks, scale, 0)

    def fold(whole):
        return (whole[:channels, :BLK] + whole[:channels, BLK:]) + (whole[channels:, :BLK] + whole[channels:, BLK:])

    def products(pair, slot):
        first, second = first_ref[pair], second_ref[pair] - (NEAR * blocks if far else 0)
        across = jnp.concatenate([buf[slot, 0], buf[slot, 1]], axis=1)
        to_second = jnp.dot(scaled[first], across, preferred_element_type=jnp.float32)
        down = jnp.concatenate(
            [jnp.concatenate([buf[slot, h, k * BLK : (k + 1) * BLK, :] for k in range(K)], axis=1) for h in range(2)],
            axis=0,
        )
        to_first = lax.dot_general(
            scaled[second], down, (((1,), (1,)), ((), ())), preferred_element_type=jnp.float32
        )
        return first, second, fold(to_first), fold(to_second)

    def add(first, second, to_first, to_second, keep):
        differs = jnp.where(first != second, keep, 0.0)
        total[first] = total[first] + to_first * keep
        total[second] = total[second] + to_second * differs

    def two(turn, carry):
        pair = start + 2 * turn
        slot = lax.rem(2 * turn, SLOTS)
        more = pair + 1 < stop
        fetch(pair, slot).wait()

        @pl.when(more)
        def _():
            fetch(pair + 1, slot + 1).wait()

        one = products(pair, slot)
        other = products(jnp.where(more, pair + 1, pair), jnp.where(more, slot + 1, slot))
        add(*one, 1.0)
        add(*other, jnp.where(more, 1.0, 0.0))
        for ahead in range(2):

            @pl.when(pair + SLOTS + ahead < stop)
            def _():
                fetch(pair + SLOTS + ahead, slot + ahead).start()

        return carry

    lax.fori_loop(0, (stop - start + 1) // 2, two, 0)
    for part in range(parts):
        for block in range(blocks):
            even, odd = pack_block(total[part * blocks + block])
            outs[part][2 * block] = even
            outs[part][2 * block + 1] = odd


def pair_messages(far, first, second, span, weights, mapped, basis, blocks):
    parts = len(mapped)
    channels = weights.shape[0]
    piece = mapped[0].shape
    return pl.pallas_call(
        functools.partial(pair_kernel, far, parts, blocks),
        out_shape=[jax.ShapeDtypeStruct(piece, jnp.float32)] * parts,
        in_specs=[pl.BlockSpec(memory_space=SMEM)] * 3
        + [pl.BlockSpec(memory_space=VMEM)] * (1 + parts)
        + [pl.BlockSpec(memory_space=pl.ANY)],
        out_specs=[pl.BlockSpec(memory_space=VMEM)] * parts,
        scratch_shapes=[
            pltpu.VMEM((K, channels, BLK), jnp.float32),
            pltpu.VMEM((parts * blocks, 2 * channels, K * BLK), jnp.bfloat16),
            pltpu.VMEM((parts * blocks, channels, BLK), jnp.float32),
            pltpu.VMEM((SLOTS, 2, K * BLK, BLK), jnp.bfloat16),
            pltpu.SemaphoreType.DMA((SLOTS,)),
        ],
        cost_estimate=pl.CostEstimate(flops=parts * 8 * K * BLK * BLK * channels * 16, transcendentals=0, bytes_accessed=parts * 8 * K * BLK * BLK * 4),
        name="pairs",
    )(first, second, span, weights, *mapped, basis)


def choose_kernel(place_ref, own_ref, beyond_ref, *outs):
    core, chip = place_ref[0], place_ref[1]
    own, beyond = own_ref[...], beyond_ref[...]
    outs[0][...] = jnp.where(core == 1, own, beyond)
    for step in range(1, len(outs)):
        outs[step][...] = jnp.where(chip >= step, own, beyond)


def chosen_blocks(place, own, beyond, steps):
    shape = jax.ShapeDtypeStruct(own.shape, jnp.float32)
    return pl.pallas_call(
        choose_kernel,
        out_shape=[shape] * steps,
        in_specs=[pl.BlockSpec(memory_space=SMEM)] + [pl.BlockSpec(memory_space=VMEM)] * 2,
        out_specs=[pl.BlockSpec(memory_space=VMEM)] * steps,
        name="chosen_blocks",
    )(place, own, beyond)


def collect_kernel(steps, place_ref, *refs):
    core, chip = place_ref[0], place_ref[1]
    first_own, second_own, beyond, partner = [ref[...] for ref in refs[:4]]
    returned = refs[4 : 4 + steps]
    own_out, beyond_out = refs[4 + steps :]
    own = first_own + second_own + jnp.where(core == 1, partner, 0.0)
    beyond = beyond + jnp.where(core == 1, 0.0, partner)
    for step in range(1, steps + 1):
        value = returned[step - 1][...]
        own = own + jnp.where(chip >= step, value, 0.0)
        beyond = beyond + jnp.where(chip >= step, 0.0, value)
    own_out[...] = own
    beyond_out[...] = beyond


def collected(place, first_own, second_own, beyond, partner, returned):
    shape = jax.ShapeDtypeStruct(first_own.shape, jnp.float32)
    return pl.pallas_call(
        functools.partial(collect_kernel, len(returned)),
        out_shape=[shape] * 2,
        in_specs=[pl.BlockSpec(memory_space=SMEM)] + [pl.BlockSpec(memory_space=VMEM)] * (4 + len(returned)),
        out_specs=[pl.BlockSpec(memory_space=VMEM)] * 2,
        name="collected",
    )(place, first_own, second_own, beyond, partner, *returned)


def product(left, right):
    (left_high, left_low), (right_high, right_low) = split(left), split(right)

    def part(a, b):
        return jnp.dot(a, b, preferred_element_type=jnp.float32)

    return part(left_high, right_high) + (part(left_high, right_low) + part(left_low, right_high))


def first_map_kernel(chan_ref, after_ref, weight_ref, gathered_ref, mapped_out, state_out):
    groups = state_out.shape[0]
    channels = gathered_ref.shape[0] // groups
    mapped = product(weight_ref[...], gathered_ref[...])
    for block in range(mapped.shape[1] // BLK):
        even, odd = pack_block(mapped[:, block * BLK : (block + 1) * BLK])
        mapped_out[2 * block] = even
        mapped_out[2 * block + 1] = odd
    chan = chan_ref[0]
    start = pl.multiple_of(chan // 2 * BLK, BLK)
    for group in range(groups):
        even, odd = pack_block(gathered_ref[group * channels : (group + 1) * channels, pl.ds(start, BLK)])
        state_out[group] = jnp.where(lax.rem(chan, 2) == 0, even, odd)


def first_map(chan, after, weight, gathered):
    channels, atoms = weight.shape[0], gathered.shape[1]
    shape = jax.ShapeDtypeStruct((atoms // 64, channels // 2, LANES), jnp.float32)
    return pl.pallas_call(
        first_map_kernel,
        out_shape=[shape, shape],
        in_specs=[pl.BlockSpec(memory_space=SMEM)] * 2 + [pl.BlockSpec(memory_space=VMEM)] * 2,
        out_specs=[pl.BlockSpec(memory_space=VMEM)] * 2,
        name="first_map",
    )(chan, after, weight, gathered)


def halves(ref, order):
    values = [ref[group] for group in order]
    turned = [pltpu.roll(value, LANES // 2, 1) for value in values]
    lower = jnp.concatenate([x for pair in zip(values, turned) for x in pair], axis=0)
    upper = jnp.concatenate([x for pair in zip(turned, values) for x in pair], axis=0)
    return lower, upper


def update_kernel(final_ref, message_ref, state_ref, weights_ref, state_out, sending_out):
    groups, part = state_out.shape[:2]
    channels = 2 * part

    def rows(start, stop):
        return jnp.concatenate([weights_ref[group, start:stop, :] for group in range(groups)], axis=0)

    lane = lax.broadcasted_iota(jnp.int32, (part, LANES), 1)
    lower, upper = halves(message_ref, range(groups))
    both = product(jnp.concatenate([lower.T, upper.T], axis=0), rows(0, channels)).T
    for group in range(groups):
        top = both[group * channels : group * channels + part, :LANES]
        bottom = both[group * channels + part : (group + 1) * channels, LANES:]
        mixed = jnp.where(lane < LANES // 2, top, bottom)
        state = state_ref[group] + mixed / (1.0 + jnp.exp(-mixed))
        state_out[group] = state
        sending_out[group] = state

    @pl.when(final_ref[0] == 0)
    def _():
        lower, upper = halves(state_out, range(groups))
        left = product(rows(channels, channels + part), lower)
        right = product(rows(channels + part, 2 * channels), upper)
        for group in range(groups):
            keep = slice(group * part, (group + 1) * part)
            sending_out[group] = jnp.where(lane < LANES // 2, left[keep], right[keep])


def update(final, message, state, weights):
    shape = jax.ShapeDtypeStruct(message.shape, jnp.float32)
    return pl.pallas_call(
        update_kernel,
        out_shape=[shape, shape],
        in_specs=[pl.BlockSpec(memory_space=SMEM)] + [pl.BlockSpec(memory_space=VMEM)] * 3,
        out_specs=[pl.BlockSpec(memory_space=VMEM)] * 2,
        name="update",
    )(final, message, state, weights)


def unpack_kernel(value_ref, out_ref):
    for block in range(out_ref.shape[1] // BLK):
        out_ref[:, block * BLK : (block + 1) * BLK] = unpack_block(value_ref[2 * block], value_ref[2 * block + 1])


def unpacked(value, shape):
    return pl.pallas_call(
        unpack_kernel,
        out_shape=jax.ShapeDtypeStruct(shape, jnp.float32),
        in_specs=[pl.BlockSpec(memory_space=VMEM)],
        out_specs=pl.BlockSpec(memory_space=VMEM),
        name="unpacked",
    )(value)


def shards(positions, features, block_counts, pair_table, in_weight, filter_weight, mix_weight):
    spatial = lax.axis_size("space")
    reach_dev = spatial // 4
    own_index = lax.axis_index("space")
    own_chan = lax.axis_index("chan")
    row, chips = reach_dev, reach_dev // 2
    core, chip = own_index % 2, (own_index % row) // 2
    place = jnp.stack([core, chip]).astype(jnp.int32)
    blocks = block_counts.shape[0]
    atoms_dev = positions.shape[1]
    gathered = lax.all_gather(features, "chan", axis=0, tiled=True)

    valid = (lax.broadcasted_iota(jnp.int32, (blocks, BLK), 1) < block_counts[:, None]).reshape(1, atoms_dev)
    geometry = jnp.concatenate([positions, valid.astype(jnp.float32)], axis=0)[None]
    three = jnp.concatenate([geometry] + [shifted(geometry, "space", -step) for step in (1, 2)], axis=0)
    everywhere = jnp.concatenate([three] + [shifted(three, "space", -step) for step in (3, 6)], axis=0)
    everywhere = everywhere[: reach_dev + 1]
    there = jnp.concatenate(
        [jnp.where(everywhere[:, 3:4] > 0.5, everywhere[:, :1], -FAR), everywhere[:, 1:]], axis=1
    )
    rows = there.reshape(reach_dev + 1, 4, blocks, BLK).transpose(0, 2, 1, 3).reshape(-1, 4, BLK)
    here = jnp.concatenate([jnp.where(valid, positions[:1], FAR), geometry[0, 1:]], axis=0)
    columns = here.reshape(4, blocks, BLK).transpose(1, 2, 0)

    pairs = pair_table.shape[1]
    ahead = (pair_table[1] // blocks - own_index) % spatial
    live = pair_table[2] > 0
    odd = jnp.where(core == 0, ahead + 1, jnp.where(ahead == reach_dev - 1, 2, ahead + 3))
    even = jnp.where(ahead == 0, 0, jnp.where(ahead == reach_dev, 1, ahead + 1))
    label = jnp.where(ahead % 2 == 1, odd, even)
    early, late = live & (label <= NEAR), live & (label > NEAR)
    before = lax.broadcasted_iota(jnp.int32, (pairs, pairs), 0) < lax.broadcasted_iota(jnp.int32, (pairs, pairs), 1)
    early_count = jnp.sum(early.astype(jnp.int32))
    count = early_count + jnp.sum(late.astype(jnp.int32))
    early_rank = jnp.sum((before & early[:, None]).astype(jnp.int32), axis=0)
    late_rank = jnp.sum((before & late[:, None]).astype(jnp.int32), axis=0) + early_count
    rank = jnp.where(early, early_rank, jnp.where(late, late_rank, pairs))
    chosen = rank[:, None] == lax.broadcasted_iota(jnp.int32, (pairs, pairs), 1)
    packed = (ahead * 16 + label) * blocks + pair_table[1] % blocks
    packed = packed * blocks + (pair_table[0] - own_index * blocks)
    packed = jnp.sum(jnp.where(chosen, packed[:, None], 0), axis=0)
    first, packed = packed % blocks, packed // blocks
    block, packed = packed % blocks, packed // blocks
    second = (packed % 16) * blocks + block
    placed = (packed // 16) * blocks + block
    counts = jnp.stack([early_count, count])
    basis, after = bases(first, placed, count.reshape(1), rows, columns)

    centre = (jnp.arange(K, dtype=jnp.float32) - MID) * step_width
    damp = jnp.exp(-gamma_width * centre * centre)
    weights = (filter_weight * damp[None, :, None]).transpose(0, 2, 1)

    chan = own_chan.astype(jnp.int32).reshape(1)
    mapped, state = first_map(chan, after, in_weight[0], gathered)
    both_weights = jnp.concatenate([mix_weight.transpose(0, 2, 1), jnp.roll(in_weight, -1, axis=0)], axis=1)

    def layer_turn(layer, carry):
        state, mapped = carry
        local = both_weights[layer]
        whole = lax.all_gather(local, "chan", axis=0, tiled=True).reshape(-1, *local.shape)
        beyond = along(mapped, lambda i: (i - row) % spatial)
        to_partner, *outgoing = chosen_blocks(place, mapped, beyond, chips)
        same = [
            along(x, lambda i, step=step: i // row * row + (i % row - 2 * step) % row)
            for step, x in enumerate(outgoing, 1)
        ]
        partner = along(to_partner, lambda i: i ^ 1)
        other = [along(x, lambda i: i ^ 1) for x in same]
        near = [mapped, beyond, partner, same[0], other[0]]
        distant = [mapped] + [x for step in range(1, chips - 1) for x in (same[step], other[step])]

        def messages(far, mapped_blocks):
            return pair_messages(
                far, first, second, counts, weights[layer], mapped_blocks, basis, blocks
            )

        near_own, to_beyond, for_partner, *near_sent = messages(0, near)
        far_own, *far_sent = messages(1, distant)
        from_partner = along(for_partner, lambda i: i ^ 1)
        both = near_sent + far_sent
        returned = []
        for step in range(1, chips):
            home = both[2 * step - 2] + along(both[2 * step - 1], lambda i: i ^ 1)
            returned.append(along(home, lambda i, step=step: i // row * row + (i % row + 2 * step) % row))
        own_sum, beyond_sum = collected(place, near_own, far_own, to_beyond, from_partner, returned)
        received = own_sum + along(beyond_sum, lambda i: (i + row) % spatial)
        message = lax.all_to_all(received, "chan", 0, 0)
        final = (layer + 1 == LAYERS).astype(jnp.int32).reshape(1)
        state, sending = update(final, message, state, whole)
        return state, lax.all_to_all(sending, "chan", 0, 0)

    state, mapped = lax.fori_loop(0, LAYERS, layer_turn, (state, mapped))
    return unpacked(mapped, features.shape)


def solution(mesh):
    placed = (
        P(None, "space"),
        P("chan", "space"),
        P("space"),
        P(None, "space"),
        P(None, "chan", None),
        P(None, None, "chan"),
        P(None, None, "chan"),
    )
    return jax.shard_map(
        shards, mesh=mesh, in_specs=placed, out_specs=P("chan", "space"), check_vma=False
    )
```

```python
import functools
import math

import jax
import jax.numpy as jnp
from jax import lax
from jax.experimental import pallas as pl
from jax.experimental.pallas import tpu as pltpu
from jax.sharding import PartitionSpec as P

K = 8
LAYERS = 2
BLK = 128
LANES = 128

cutoff_radius = 6.0
gamma_width = 1.5
step_width = cutoff_radius / (K - 1)
MID = 4
FAR = 1000.0
SLOTS = 6
NEAR = 4

ENVELOPE = (
    0.02777777772845049,
    -0.00018032445737786967,
    4.2799604015759175e-07,
    -5.319790167613903e-10,
    3.90316047548473e-13,
)

VMEM = pltpu.MemorySpace.VMEM
SMEM = pltpu.MemorySpace.SMEM


def shifted(block, axis, distance):
    devices = range(lax.axis_size(axis))
    route = [((i - distance) % len(devices), i) for i in devices]
    return lax.ppermute(block, axis, route)


def along(block, target):
    return lax.ppermute(block, "space", [(i, target(i)) for i in range(lax.axis_size("space"))])


def split(value):
    high = value.astype(jnp.bfloat16)
    low = (value - high.astype(jnp.float32)).astype(jnp.bfloat16)
    return high, low


def basis_kernel(first_ref, second_ref, count_ref, rows_ref, columns_ref, out_ref, done_ref, wide, buf, sem):
    done_ref[0] = 1
    blocks = columns_ref.shape[0]
    for block in range(blocks):
        for axis in range(3):
            wide[block * 3 + axis] = jnp.broadcast_to(columns_ref[block, :, axis : axis + 1], (BLK, BLK))
    count = count_ref[0]
    chunk = 32

    def one(pair, carry):
        slot = lax.rem(pair, SLOTS)

        @pl.when(pair >= SLOTS)
        def _():
            pltpu.make_async_copy(buf.at[slot], out_ref.at[pair - SLOTS], sem.at[slot]).wait()

        first, second = first_ref[pair], second_ref[pair]
        same = (first == second).astype(jnp.float32)
        for part in range(BLK // chunk):
            rows = slice(part * chunk, (part + 1) * chunk)
            squared = None
            for axis in range(3):
                offset = wide[first * 3 + axis, rows, :] - rows_ref[second, axis : axis + 1, :]
                squared = offset * offset if squared is None else squared + offset * offset
            here = lax.broadcasted_iota(jnp.int32, (chunk, BLK), 0) + part * chunk
            there = lax.broadcasted_iota(jnp.int32, (chunk, BLK), 1)
            squared = squared + jnp.where(here == there, same * FAR, 0.0)
            squared = jnp.minimum(squared, cutoff_radius * cutoff_radius)
            distance = squared * lax.rsqrt(jnp.maximum(squared, 1e-20))
            bell = ENVELOPE[4]
            for power in (3, 2, 1, 0):
                bell = bell * squared + ENVELOPE[power]
            bell = bell * (cutoff_radius * cutoff_radius - squared)
            bell = bell * bell
            away = distance - MID * step_width
            middle = bell * jnp.exp(away * away * -gamma_width)
            up = jnp.exp(away * (2.0 * gamma_width * step_width))
            down = jnp.exp(away * (-2.0 * gamma_width * step_width))

            def keep(k, value):
                high, low = split(value)
                buf[slot, 0, k * BLK + part * chunk : k * BLK + (part + 1) * chunk, :] = high
                buf[slot, 1, k * BLK + part * chunk : k * BLK + (part + 1) * chunk, :] = low

            keep(MID, middle)
            value = middle
            for k in range(MID + 1, K):
                value = value * up
                keep(k, value)
            value = middle
            for k in range(MID - 1, -1, -1):
                value = value * down
                keep(k, value)
        pltpu.make_async_copy(buf.at[slot], out_ref.at[pair], sem.at[slot]).start()
        return carry

    lax.fori_loop(0, count, one, 0)

    for slot in range(SLOTS):

        @pl.when(slot < count)
        def _():
            pltpu.make_async_copy(buf.at[slot], out_ref.at[slot], sem.at[slot]).wait()


def bases(first, second, count, rows, columns):
    pairs = first.shape[0]
    blocks = columns.shape[0]
    return pl.pallas_call(
        basis_kernel,
        out_shape=[
            jax.ShapeDtypeStruct((pairs, 2, K * BLK, BLK), jnp.bfloat16),
            jax.ShapeDtypeStruct((1,), jnp.int32),
        ],
        in_specs=[pl.BlockSpec(memory_space=SMEM)] * 3 + [pl.BlockSpec(memory_space=VMEM)] * 2,
        out_specs=[pl.BlockSpec(memory_space=pl.ANY), pl.BlockSpec(memory_space=SMEM)],
        scratch_shapes=[
            pltpu.VMEM((blocks * 3, BLK, BLK), jnp.float32),
            pltpu.VMEM((SLOTS, 2, K * BLK, BLK), jnp.bfloat16),
            pltpu.SemaphoreType.DMA((SLOTS,)),
        ],
        cost_estimate=pl.CostEstimate(flops=pairs * K * BLK * BLK * 10, transcendentals=pairs * BLK * BLK * 4, bytes_accessed=pairs * K * BLK * BLK * 4),
        name="bases",
    )(first, second, count, rows, columns)


def unpack_block(even, odd):
    lane = lax.broadcasted_iota(jnp.int32, even.shape, 1)
    half = LANES // 2
    top = jnp.where(lane < half, even, pltpu.roll(odd, half, 1))
    bottom = jnp.where(lane < half, pltpu.roll(even, half, 1), odd)
    return jnp.concatenate([top, bottom], axis=0)


def pack_block(block):
    channels = block.shape[0]
    top, bottom = block[: channels // 2], block[channels // 2 :]
    lane = lax.broadcasted_iota(jnp.int32, top.shape, 1)
    half = LANES // 2
    even = jnp.where(lane < half, top, pltpu.roll(bottom, half, 1))
    odd = jnp.where(lane < half, pltpu.roll(top, half, 1), bottom)
    return even, odd


def pair_kernel(far, parts, blocks, *refs):
    first_ref, second_ref, count_ref, weight_ref = refs[:4]
    mapped = refs[4 : 4 + parts]
    basis_ref = refs[4 + parts]
    outs = refs[5 + parts : 5 + 2 * parts]
    wide, scaled, total, buf, sem = refs[5 + 2 * parts :]
    channels = total.shape[1]
    start, stop = (count_ref[0], count_ref[1]) if far else (0, count_ref[0])

    def fetch(pair, slot):
        return pltpu.make_async_copy(basis_ref.at[pair], buf.at[slot], sem.at[slot])

    for early in range(SLOTS):

        @pl.when(start + early < stop)
        def _():
            fetch(start + early, early).start()

    for k in range(K):
        wide[k] = jnp.broadcast_to(weight_ref[:, k : k + 1], wide.shape[1:])
    for part in range(parts):
        for block in range(blocks):
            total[part * blocks + block] = unpack_block(mapped[part][2 * block], mapped[part][2 * block + 1])

    def scale(block, carry):
        feature = total[block]
        for k in range(K):
            high, low = split(feature * wide[k])
            scaled[block, :channels, k * BLK : (k + 1) * BLK] = high
            scaled[block, channels:, k * BLK : (k + 1) * BLK] = low
        total[block] = jnp.zeros_like(feature)
        return carry

    lax.fori_loop(0, parts * blocks, scale, 0)

    def fold(whole):
        return (whole[:channels, :BLK] + whole[:channels, BLK:]) + (whole[channels:, :BLK] + whole[channels:, BLK:])

    def products(pair, slot):
        first, second = first_ref[pair], second_ref[pair] - (NEAR * blocks if far else 0)
        across = jnp.concatenate([buf[slot, 0], buf[slot, 1]], axis=1)
        to_second = jnp.dot(scaled[first], across, preferred_element_type=jnp.float32)
        down = jnp.concatenate(
            [jnp.concatenate([buf[slot, h, k * BLK : (k + 1) * BLK, :] for k in range(K)], axis=1) for h in range(2)],
            axis=0,
        )
        to_first = lax.dot_general(
            scaled[second], down, (((1,), (1,)), ((), ())), preferred_element_type=jnp.float32
        )
        return first, second, fold(to_first), fold(to_second)

    def add(first, second, to_first, to_second, keep):
        differs = jnp.where(first != second, keep, 0.0)
        total[first] = total[first] + to_first * keep
        total[second] = total[second] + to_second * differs

    def two(turn, carry):
        pair = start + 2 * turn
        slot = lax.rem(2 * turn, SLOTS)
        more = pair + 1 < stop
        fetch(pair, slot).wait()

        @pl.when(more)
        def _():
            fetch(pair + 1, slot + 1).wait()

        one = products(pair, slot)
        other = products(jnp.where(more, pair + 1, pair), jnp.where(more, slot + 1, slot))
        add(*one, 1.0)
        add(*other, jnp.where(more, 1.0, 0.0))
        for ahead in range(2):

            @pl.when(pair + SLOTS + ahead < stop)
            def _():
                fetch(pair + SLOTS + ahead, slot + ahead).start()

        return carry

    lax.fori_loop(0, (stop - start + 1) // 2, two, 0)
    for part in range(parts):
        for block in range(blocks):
            even, odd = pack_block(total[part * blocks + block])
            outs[part][2 * block] = even
            outs[part][2 * block + 1] = odd


def pair_messages(far, first, second, span, weights, mapped, basis, blocks):
    parts = len(mapped)
    channels = weights.shape[0]
    piece = mapped[0].shape
    return pl.pallas_call(
        functools.partial(pair_kernel, far, parts, blocks),
        out_shape=[jax.ShapeDtypeStruct(piece, jnp.float32)] * parts,
        in_specs=[pl.BlockSpec(memory_space=SMEM)] * 3
        + [pl.BlockSpec(memory_space=VMEM)] * (1 + parts)
        + [pl.BlockSpec(memory_space=pl.ANY)],
        out_specs=[pl.BlockSpec(memory_space=VMEM)] * parts,
        scratch_shapes=[
            pltpu.VMEM((K, channels, BLK), jnp.float32),
            pltpu.VMEM((parts * blocks, 2 * channels, K * BLK), jnp.bfloat16),
            pltpu.VMEM((parts * blocks, channels, BLK), jnp.float32),
            pltpu.VMEM((SLOTS, 2, K * BLK, BLK), jnp.bfloat16),
            pltpu.SemaphoreType.DMA((SLOTS,)),
        ],
        cost_estimate=pl.CostEstimate(flops=parts * 8 * K * BLK * BLK * channels * 16, transcendentals=0, bytes_accessed=parts * 8 * K * BLK * BLK * 4),
        name="pairs",
    )(first, second, span, weights, *mapped, basis)


def choose_kernel(place_ref, own_ref, beyond_ref, *outs):
    core, chip = place_ref[0], place_ref[1]
    own, beyond = own_ref[...], beyond_ref[...]
    outs[0][...] = jnp.where(core == 1, own, beyond)
    for step in range(1, len(outs)):
        outs[step][...] = jnp.where(chip >= step, own, beyond)


def chosen_blocks(place, own, beyond, steps):
    shape = jax.ShapeDtypeStruct(own.shape, jnp.float32)
    return pl.pallas_call(
        choose_kernel,
        out_shape=[shape] * steps,
        in_specs=[pl.BlockSpec(memory_space=SMEM)] + [pl.BlockSpec(memory_space=VMEM)] * 2,
        out_specs=[pl.BlockSpec(memory_space=VMEM)] * steps,
        name="chosen_blocks",
    )(place, own, beyond)


def collect_kernel(steps, place_ref, *refs):
    core, chip = place_ref[0], place_ref[1]
    first_own, second_own, beyond, partner = [ref[...] for ref in refs[:4]]
    returned = refs[4 : 4 + steps]
    own_out, beyond_out = refs[4 + steps :]
    own = first_own + second_own + jnp.where(core == 1, partner, 0.0)
    beyond = beyond + jnp.where(core == 1, 0.0, partner)
    for step in range(1, steps + 1):
        value = returned[step - 1][...]
        own = own + jnp.where(chip >= step, value, 0.0)
        beyond = beyond + jnp.where(chip >= step, 0.0, value)
    own_out[...] = own
    beyond_out[...] = beyond


def collected(place, first_own, second_own, beyond, partner, returned):
    shape = jax.ShapeDtypeStruct(first_own.shape, jnp.float32)
    return pl.pallas_call(
        functools.partial(collect_kernel, len(returned)),
        out_shape=[shape] * 2,
        in_specs=[pl.BlockSpec(memory_space=SMEM)] + [pl.BlockSpec(memory_space=VMEM)] * (4 + len(returned)),
        out_specs=[pl.BlockSpec(memory_space=VMEM)] * 2,
        name="collected",
    )(place, first_own, second_own, beyond, partner, *returned)


def product(left, right):
    (left_high, left_low), (right_high, right_low) = split(left), split(right)

    def part(a, b):
        return jnp.dot(a, b, preferred_element_type=jnp.float32)

    return part(left_high, right_high) + (part(left_high, right_low) + part(left_low, right_high))


def first_map_kernel(chan_ref, after_ref, weight_ref, gathered_ref, mapped_out, state_out):
    groups = state_out.shape[0]
    channels = gathered_ref.shape[0] // groups
    mapped = product(weight_ref[...], gathered_ref[...])
    for block in range(mapped.shape[1] // BLK):
        even, odd = pack_block(mapped[:, block * BLK : (block + 1) * BLK])
        mapped_out[2 * block] = even
        mapped_out[2 * block + 1] = odd
    chan = chan_ref[0]
    start = pl.multiple_of(chan // 2 * BLK, BLK)
    for group in range(groups):
        even, odd = pack_block(gathered_ref[group * channels : (group + 1) * channels, pl.ds(start, BLK)])
        state_out[group] = jnp.where(lax.rem(chan, 2) == 0, even, odd)


def first_map(chan, after, weight, gathered):
    channels, atoms = weight.shape[0], gathered.shape[1]
    shape = jax.ShapeDtypeStruct((atoms // 64, channels // 2, LANES), jnp.float32)
    return pl.pallas_call(
        first_map_kernel,
        out_shape=[shape, shape],
        in_specs=[pl.BlockSpec(memory_space=SMEM)] * 2 + [pl.BlockSpec(memory_space=VMEM)] * 2,
        out_specs=[pl.BlockSpec(memory_space=VMEM)] * 2,
        name="first_map",
    )(chan, after, weight, gathered)


def halves(ref, order):
    values = [ref[group] for group in order]
    turned = [pltpu.roll(value, LANES // 2, 1) for value in values]
    lower = jnp.concatenate([x for pair in zip(values, turned) for x in pair], axis=0)
    upper = jnp.concatenate([x for pair in zip(turned, values) for x in pair], axis=0)
    return lower, upper


def update_kernel(final_ref, message_ref, state_ref, weights_ref, state_out, sending_out):
    groups, part = state_out.shape[:2]
    channels = 2 * part

    def rows(start, stop):
        return jnp.concatenate([weights_ref[group, start:stop, :] for group in range(groups)], axis=0)

    lane = lax.broadcasted_iota(jnp.int32, (part, LANES), 1)
    lower, upper = halves(message_ref, range(groups))
    both = product(jnp.concatenate([lower.T, upper.T], axis=0), rows(0, channels)).T
    for group in range(groups):
        top = both[group * channels : group * channels + part, :LANES]
        bottom = both[group * channels + part : (group + 1) * channels, LANES:]
        mixed = jnp.where(lane < LANES // 2, top, bottom)
        state = state_ref[group] + mixed / (1.0 + jnp.exp(-mixed))
        state_out[group] = state
        sending_out[group] = state

    @pl.when(final_ref[0] == 0)
    def _():
        lower, upper = halves(state_out, range(groups))
        left = product(rows(channels, channels + part), lower)
        right = product(rows(channels + part, 2 * channels), upper)
        for group in range(groups):
            keep = slice(group * part, (group + 1) * part)
            sending_out[group] = jnp.where(lane < LANES // 2, left[keep], right[keep])


def update(final, message, state, weights):
    shape = jax.ShapeDtypeStruct(message.shape, jnp.float32)
    return pl.pallas_call(
        update_kernel,
        out_shape=[shape, shape],
        in_specs=[pl.BlockSpec(memory_space=SMEM)] + [pl.BlockSpec(memory_space=VMEM)] * 3,
        out_specs=[pl.BlockSpec(memory_space=VMEM)] * 2,
        name="update",
    )(final, message, state, weights)


def unpack_kernel(value_ref, out_ref):
    for block in range(out_ref.shape[1] // BLK):
        out_ref[:, block * BLK : (block + 1) * BLK] = unpack_block(value_ref[2 * block], value_ref[2 * block + 1])


def unpacked(value, shape):
    return pl.pallas_call(
        unpack_kernel,
        out_shape=jax.ShapeDtypeStruct(shape, jnp.float32),
        in_specs=[pl.BlockSpec(memory_space=VMEM)],
        out_specs=pl.BlockSpec(memory_space=VMEM),
        name="unpacked",
    )(value)


def shards(positions, features, block_counts, pair_table, in_weight, filter_weight, mix_weight):
    spatial = lax.axis_size("space")
    reach_dev = spatial // 4
    own_index = lax.axis_index("space")
    own_chan = lax.axis_index("chan")
    row, chips = reach_dev, reach_dev // 2
    core, chip = own_index % 2, (own_index % row) // 2
    place = jnp.stack([core, chip]).astype(jnp.int32)
    blocks = block_counts.shape[0]
    atoms_dev = positions.shape[1]
    gathered = lax.all_gather(features, "chan", axis=0, tiled=True)

    valid = (lax.broadcasted_iota(jnp.int32, (blocks, BLK), 1) < block_counts[:, None]).reshape(1, atoms_dev)
    geometry = jnp.concatenate([positions, valid.astype(jnp.float32)], axis=0)[None]
    three = jnp.concatenate([geometry] + [shifted(geometry, "space", -step) for step in (1, 2)], axis=0)
    everywhere = jnp.concatenate([three] + [shifted(three, "space", -step) for step in (3, 6)], axis=0)
    everywhere = everywhere[: reach_dev + 1]
    there = jnp.concatenate(
        [jnp.where(everywhere[:, 3:4] > 0.5, everywhere[:, :1], -FAR), everywhere[:, 1:]], axis=1
    )
    rows = there.reshape(reach_dev + 1, 4, blocks, BLK).transpose(0, 2, 1, 3).reshape(-1, 4, BLK)
    here = jnp.concatenate([jnp.where(valid, positions[:1], FAR), geometry[0, 1:]], axis=0)
    columns = here.reshape(4, blocks, BLK).transpose(1, 2, 0)

    pairs = pair_table.shape[1]
    ahead = (pair_table[1] // blocks - own_index) % spatial
    live = pair_table[2] > 0
    odd = jnp.where(core == 0, ahead + 1, jnp.where(ahead == reach_dev - 1, 2, ahead + 3))
    even = jnp.where(ahead == 0, 0, jnp.where(ahead == reach_dev, 1, ahead + 1))
    label = jnp.where(ahead % 2 == 1, odd, even)
    early, late = live & (label <= NEAR), live & (label > NEAR)
    before = lax.broadcasted_iota(jnp.int32, (pairs, pairs), 0) < lax.broadcasted_iota(jnp.int32, (pairs, pairs), 1)
    early_count = jnp.sum(early.astype(jnp.int32))
    count = early_count + jnp.sum(late.astype(jnp.int32))
    early_rank = jnp.sum((before & early[:, None]).astype(jnp.int32), axis=0)
    late_rank = jnp.sum((before & late[:, None]).astype(jnp.int32), axis=0) + early_count
    rank = jnp.where(early, early_rank, jnp.where(late, late_rank, pairs))
    chosen = rank[:, None] == lax.broadcasted_iota(jnp.int32, (pairs, pairs), 1)
    packed = (ahead * 16 + label) * blocks + pair_table[1] % blocks
    packed = packed * blocks + (pair_table[0] - own_index * blocks)
    packed = jnp.sum(jnp.where(chosen, packed[:, None], 0), axis=0)
    first, packed = packed % blocks, packed // blocks
    block, packed = packed % blocks, packed // blocks
    second = (packed % 16) * blocks + block
    placed = (packed // 16) * blocks + block
    counts = jnp.stack([early_count, count])
    basis, after = bases(first, placed, count.reshape(1), rows, columns)

    centre = (jnp.arange(K, dtype=jnp.float32) - MID) * step_width
    damp = jnp.exp(-gamma_width * centre * centre)
    weights = (filter_weight * damp[None, :, None]).transpose(0, 2, 1)

    chan = own_chan.astype(jnp.int32).reshape(1)
    mapped, state = first_map(chan, after, in_weight[0], gathered)
    both_weights = jnp.concatenate([mix_weight.transpose(0, 2, 1), jnp.roll(in_weight, -1, axis=0)], axis=1)

    def layer_turn(layer, carry):
        state, mapped = carry
        local = both_weights[layer]
        whole = lax.all_gather(local, "chan", axis=0, tiled=True).reshape(-1, *local.shape)
        beyond = along(mapped, lambda i: (i - row) % spatial)
        to_partner = jnp.where(core == 1, mapped, beyond)
        outgoing = [jnp.where(chip >= step, mapped, beyond) for step in range(1, chips)]
        same = [
            along(x, lambda i, step=step: i // row * row + (i % row - 2 * step) % row)
            for step, x in enumerate(outgoing, 1)
        ]
        partner = along(to_partner, lambda i: i ^ 1)
        other = [along(x, lambda i: i ^ 1) for x in same]
        near = [mapped, beyond, partner, same[0], other[0]]
        distant = [mapped] + [x for step in range(1, chips - 1) for x in (same[step], other[step])]

        def messages(far, mapped_blocks):
            return pair_messages(
                far, first, second, counts, weights[layer], mapped_blocks, basis, blocks
            )

        near_own, to_beyond, for_partner, *near_sent = messages(0, near)
        far_own, *far_sent = messages(1, distant)
        from_partner = along(for_partner, lambda i: i ^ 1)
        both = near_sent + far_sent
        returned = []
        for step in range(1, chips):
            home = both[2 * step - 2] + along(both[2 * step - 1], lambda i: i ^ 1)
            returned.append(along(home, lambda i, step=step: i // row * row + (i % row + 2 * step) % row))
        own_sum, beyond_sum = collected(place, near_own, far_own, to_beyond, from_partner, returned)
        received = own_sum + along(beyond_sum, lambda i: (i + row) % spatial)
        message = lax.all_to_all(received, "chan", 0, 0)
        final = (layer + 1 == LAYERS).astype(jnp.int32).reshape(1)
        state, sending = update(final, message, state, whole)
        return state, lax.all_to_all(sending, "chan", 0, 0)

    state, mapped = lax.fori_loop(0, LAYERS, layer_turn, (state, mapped))
    return unpacked(mapped, features.shape)


def solution(mesh):
    placed = (
        P(None, "space"),
        P("chan", "space"),
        P("space"),
        P(None, "space"),
        P(None, "chan", None),
        P(None, None, "chan"),
        P(None, None, "chan"),
    )
    return jax.shard_map(
        shards, mesh=mesh, in_specs=placed, out_specs=P("chan", "space"), check_vma=False
    )
```
